32 devices in a mesh: dp: 8 (over z, y), tensor: 4 (over x, core).
Axes of the slice: x: 2, y: 2, z: 4, core: 2. Of those that a mesh axis runs over, the one named last changes fastest.
Arguments:
- states: bfloat16 [4, 1024, 5120], P(None, 'dp', 'tensor'), may hold values from -6 to 6
- mix_weights: float32 [4], replicated, may hold values from 0.3 to 1
- router: bfloat16 [5120], P('tensor'), may hold values from -0.078125 to 0.078125
- norm_gain: bfloat16 [5120], P('tensor'), may hold values from 0.5 to 1.5
- gate_weight: bfloat16 [5120, 6912], P('tensor', 'dp'), may hold values from -0.078125 to 0.078125
- up_weight: bfloat16 [5120, 6912], P('tensor', 'dp'), may hold values from -0.078125 to 0.078125
- down_weight: bfloat16 [6912, 5120], P('dp', 'tensor'), may hold values from -0.078125 to 0.078125
- counts: int32 [1, 8], replicated, may hold values from 1 to 24, 128 in all within a row
- chosen: int32 [8, 24], P('dp'), may hold values from 0 to 127, as said below
- cotangent: bfloat16 [1024, 5120], P('dp', 'tensor'), may hold values from -6 to 6
Outputs:
- updated: bfloat16 [1024, 5120], P('dp', 'tensor')
- grad_input: bfloat16 [1024, 5120], P('dp', 'tensor')
- grad_gate: float32 [5120, 6912], P('tensor', 'dp')
- grad_up: float32 [5120, 6912], P('tensor', 'dp')
- grad_down: float32 [6912, 5120], P('dp', 'tensor')
The draws below stay inside these ranges and needn't reach their ends.
Inputs may be any that keep to these rules, and one draw needn't show every extreme that they name: Each row of counts sums to one eighth of 1024; entry [s, j] belongs to index s * 8 + j of dp. `chosen`: each row holds 24 distinct positions; the first counts entries of row p are the selected tokens of index p of dp, the rest are padding.
All inputs are finite; a program needn't handle non-finite values.
Results may differ from the reference program's by a relative error of at most 0.014.
Values may be sent and summed in bfloat16 or wider, within the bound.
No kernel may reach another device: no remote copies, remote signals or barrier semaphores. Data moves between devices by JAX's collectives and lax.ppermute only.
A program may use at most 128 MiB of HBM per device.

```python
import math
import jax
import jax.numpy as jnp
import numpy as np
from jax import lax

D = 5120
FF = 6912
DEPTH = 4
SEQ = 1024
TOK_DEV = 128
SPAN = 8
SHARE = 16
CAP = 24
RANKS = 8
NSEQ = 1
TOKENS = 1024


def draw_chosen(key, part):
    keys = jax.random.split(key, RANKS)

    def one_row(row_key):
        return jax.random.permutation(row_key, TOK_DEV)[:CAP].astype(jnp.int32)
    table = jax.vmap(one_row)(keys).astype(jnp.int32)
    first_row = table[0]
    first_row = ((first_row + (TOK_DEV - 1 - first_row[0])) % TOK_DEV).astype(jnp.int32)
    return table.at[0].set(first_row)


def levels(key, dims, pieces, low, largest):
    gain, own = 1.0, jax.random.fold_in(key, 6)
    for dim, shards_of in pieces:
        draws = jnp.exp(jax.random.uniform(jax.random.fold_in(own, dim), (shards_of,), jnp.float32, low / len(pieces), largest / len(pieces)))
        gain = gain * jnp.repeat(draws, dims[dim] // shards_of).reshape([-1 if axis == dim else 1 for axis in range(len(dims))])
    return gain


def length_profile(amount, total, limit, lean):
    loads = [(1 << 20) // math.isqrt(standing ** lean) + 1 for standing in range(2, amount + 1)]
    rest, given = total - limit - (amount - 1), [1] * (amount - 1)
    while rest > 0:
        free = [i for i in range(amount - 1) if given[i] < limit]
        pool, left = sum([loads[i] for i in free]), rest
        for i in free:
            extra = min(limit - given[i], max(1, left * loads[i] // pool), rest)
            given[i] = given[i] + extra
            rest = rest - extra
    return np.array([limit] + given)


def ragged_sizes(rng, number_of, total, most, skew):
    if number_of == 2:
        one = jax.random.randint(rng, (), max(1, total - most), min(most, total - 1) + 1)
        return jnp.stack([one, total - one])
    lengths = jnp.asarray(length_profile(number_of, total, most, skew), jnp.int32)
    pairs = (number_of - 1) // 2
    source_of, sink = lengths[1:1 + 2 * pairs:2], lengths[2:2 + 2 * pairs:2]
    room = jnp.minimum(source_of - 1, most - sink)
    shifted = jax.random.randint(jax.random.fold_in(rng, 1), (pairs,), 0, 1 << 20) % (room + 1)
    lengths = lengths.at[1:1 + 2 * pairs:2].set(source_of - shifted).at[2:2 + 2 * pairs:2].set(sink + shifted)
    return lengths[jax.random.permutation(jax.random.fold_in(rng, 2), number_of)]


def normal_values(rng, shape, scale, most, cuts=(), kind=jnp.bfloat16):
    entries = jax.random.normal(rng, shape, jnp.float32) * scale
    if len(cuts) > 0:
        entries = levels(rng, shape, cuts, -0.22, 0.18) * entries
    return jnp.clip(entries, min=-most, max=most).astype(kind)


def setup_inputs(seed: int = 0) -> dict:
    key_of = jax.random.split(jax.random.key(seed), 11)
    return {
        "states": normal_values(key_of[0], (DEPTH, TOKENS, D), 1.0, 6.0, ((1, 8), (2, 4))),
        "mix_weights": jnp.clip(jax.random.uniform(key_of[1], (DEPTH,), jnp.float32, 0.3, 1.0), 0.3, 1.0),
        "router": normal_values(key_of[2], (D,), D ** -0.5, 0.078125, ((0, 4),)),
        "norm_gain": jnp.clip(1.0 + 0.1 * jax.random.normal(key_of[3], (D,), jnp.float32), 0.5, 1.5).astype(jnp.bfloat16),
        "gate_weight": normal_values(key_of[4], (D, FF), D ** -0.5, 0.078125, ((0, 4), (1, 8))),
        "up_weight": normal_values(key_of[5], (D, FF), D ** -0.5, 0.078125, ((0, 4), (1, 8))),
        "down_weight": normal_values(key_of[6], (FF, D), FF ** -0.5, 0.078125, ((0, 8), (1, 4))),
        "counts": jax.vmap(lambda own: ragged_sizes(own, SPAN, SEQ // 8, CAP, 2))(jax.random.split(key_of[7], NSEQ)).reshape((NSEQ, SPAN)).astype(jnp.int32),
        "chosen": draw_chosen(jax.random.fold_in(key_of[10], 71), 0),
        "cotangent": normal_values(key_of[9], (TOKENS, D), 1.0, 6.0, ((0, 8), (1, 4))),
    }


epsilon = 1e-05

def reference(states, mix_weights, router, norm_gain, gate_weight, up_weight, down_weight, counts, chosen, cotangent):
    mixed = jnp.tensordot(mix_weights, states.astype(jnp.float32), axes=1)
    flat_counts = counts.reshape(-1).astype(jnp.int32)
    slot_ids = jnp.arange(CAP).astype(jnp.int32)
    starts = (jnp.cumsum(flat_counts) - flat_counts).astype(jnp.int32)
    is_valid = slot_ids[None, :] < flat_counts[:, None]
    global_rank = (starts[:, None] + slot_ids[None, :]).astype(jnp.int32)
    total_rows = RANKS * SHARE
    target = jnp.where(is_valid, global_rank, total_rows).astype(jnp.int32)
    token_ids = (jnp.arange(RANKS).astype(jnp.int32)[:, None] * TOK_DEV + chosen).astype(jnp.int32)
    packed = jnp.zeros((total_rows,), jnp.int32).at[target.reshape(-1)].set(token_ids.reshape(-1), mode='drop')
    picked = mixed[packed]
    router_float = router.astype(jnp.float32)
    gain_float = norm_gain.astype(jnp.float32)
    logits = lax.optimization_barrier(jnp.sum(picked * router_float, axis=1))
    gating = jax.nn.sigmoid(logits)
    inverse = lax.rsqrt(lax.optimization_barrier(jnp.mean(picked * picked, axis=1)) + epsilon)
    normed = (picked * inverse[:, None] * gain_float).astype(jnp.bfloat16)
    gate_pre = jnp.dot(normed, gate_weight, preferred_element_type=jnp.float32)
    up_pre = jnp.dot(normed, up_weight, preferred_element_type=jnp.float32)
    hidden = (jax.nn.silu(gate_pre) * up_pre).astype(jnp.bfloat16)
    update = jnp.dot(hidden, down_weight, preferred_element_type=jnp.float32).astype(jnp.bfloat16)
    new_rows = picked + gating[:, None] * update.astype(jnp.float32)
    updated = mixed.at[packed].set(new_rows).astype(jnp.bfloat16)
    cot_rows = cotangent.astype(jnp.float32)[packed]
    dupdate = (gating[:, None] * cot_rows).astype(jnp.bfloat16)
    dlogit = gating * (1.0 - gating) * lax.optimization_barrier(jnp.sum(cot_rows * update.astype(jnp.float32), axis=1))
    dhidden = jnp.dot(dupdate, down_weight.T, preferred_element_type=jnp.float32)
    sigmoid_pre = jax.nn.sigmoid(gate_pre)
    dgate = (dhidden * up_pre * sigmoid_pre * (1.0 + gate_pre * (1.0 - sigmoid_pre))).astype(jnp.bfloat16)
    dup = (dhidden * gate_pre * sigmoid_pre).astype(jnp.bfloat16)
    grad_down = jnp.dot(hidden.T, dupdate, preferred_element_type=jnp.float32)
    grad_gate = jnp.dot(normed.T, dgate, preferred_element_type=jnp.float32)
    grad_up = jnp.dot(normed.T, dup, preferred_element_type=jnp.float32)
    dnormed = jnp.dot(dgate, gate_weight.T, preferred_element_type=jnp.float32) + jnp.dot(dup, up_weight.T, preferred_element_type=jnp.float32)
    scaled = dnormed * gain_float
    inner = lax.optimization_barrier(jnp.mean(scaled * picked, axis=1))
    drows = cot_rows + inverse[:, None] * scaled - picked * (inverse ** 3 * inner)[:, None] + dlogit[:, None] * router_float
    grad_input = cotangent.astype(jnp.float32).at[packed].set(drows).astype(jnp.bfloat16)
    return (updated, grad_input, grad_gate, grad_up, grad_down)
```

```python
import functools
import jax
import jax.numpy as jnp
from jax import lax
from jax.experimental import pallas as pl
from jax.experimental.pallas import tpu as pltpu
from jax.sharding import PartitionSpec as P

epsilon = 1e-05
f32, bf16 = jnp.float32, jnp.bfloat16
SMEM = pl.BlockSpec(memory_space=pltpu.SMEM)
VMEM = pl.BlockSpec(memory_space=pltpu.VMEM)
PARTS = 3


def call(kernel, out, ins, scratch=(), flops=0, nbytes=0, vmem=32 << 20):
    return pl.pallas_call(
        kernel,
        out_shape=out,
        in_specs=ins,
        out_specs=jax.tree.map(lambda _: VMEM, out),
        scratch_shapes=list(scratch),
        cost_estimate=pl.CostEstimate(flops=flops, bytes_accessed=nbytes, transcendentals=0),
        compiler_params=pltpu.CompilerParams(vmem_limit_bytes=vmem),
    )


def sds(shape, dtype):
    return jax.ShapeDtypeStruct(shape, dtype)


def terms(value):
    out, rest = [], value
    for _ in range(PARTS):
        term = rest.astype(bf16).astype(f32)
        out.append(term)
        rest = rest - term
    return out


def in_lanes(values, width, first):
    rows = values[0].shape[0]
    lane = lax.broadcasted_iota(jnp.int32, (rows, width), 1)
    total = jnp.zeros((rows, width), f32)
    for i, value in enumerate(values):
        total = jnp.where(lane == first + i, value, total)
    return total


def dot_nt(a, b):
    return lax.dot_general(a, b, (((1,), (1,)), ((), ())), preferred_element_type=f32)


def dot_nn(a, b):
    return jnp.dot(a, b, preferred_element_type=f32)


def placement(counts_ref, me, slots, slot_rows, total, packed_axis):
    shape = (total, slots * slot_rows) if packed_axis == 0 else (slots * slot_rows, total)
    packed = lax.broadcasted_iota(jnp.int32, shape, packed_axis)
    slotted = lax.broadcasted_iota(jnp.int32, shape, 1 - packed_axis)
    hit, at = packed < 0, 0
    for k in range(slots):
        here = counts_ref[0, me ^ k]
        row = slotted - k * slot_rows
        hit = hit | ((row >= 0) & (row < here) & (packed == row + at))
        at = at + here
    return jnp.where(hit, 1.0, 0.0).astype(bf16)


def pick_kernel(cap, chosen, mixw, states, cot, router, gain, picked_ref, load_ref):
    tokens, width = cot.shape
    row = lax.broadcasted_iota(jnp.int32, (cap, tokens), 0)
    col = lax.broadcasted_iota(jnp.int32, (cap, tokens), 1)
    want = jnp.zeros((cap, tokens), f32)
    for k in range(cap):
        want = jnp.where((row == k) & (col == chosen[0, k]), 1.0, want)
    want = want.astype(bf16)
    picked = mixw[0] * dot_nn(want, states[0])
    for j in range(1, states.shape[0]):
        picked = picked + mixw[j] * dot_nn(want, states[j])
    picked_ref[...] = picked
    load_ref[:, :width] = (picked * gain[...].astype(f32)).astype(bf16)
    load_ref[:, width : 2 * width] = dot_nn(want, cot[...]).astype(bf16)
    logit = jnp.sum(picked * router[...].astype(f32), axis=1, keepdims=True)
    square = jnp.sum(picked * picked, axis=1, keepdims=True)
    first = 2 * PARTS * lax.axis_index("tensor")
    load_ref[:, 2 * width :] = in_lanes(terms(logit) + terms(square), 128, first).astype(bf16)


def first_kernel(slots, cap, slot_rows, lanes, counts, *refs):
    blocks = refs[:slots]
    gate_w, up_w, down_w, own_ref, send_ref, pg_ref, cot_ref, rows_ref, sums_ref = refs[slots:]
    me = lax.axis_index("dp")
    core = lax.axis_index("tensor") % 2
    width, ff = gate_w.shape
    total = pg_ref.shape[0]
    for k in range(slots):
        rows_ref[k * slot_rows : k * slot_rows + cap, :] = blocks[k][...]
        rows_ref[k * slot_rows + cap : (k + 1) * slot_rows, :] = jnp.zeros((slot_rows - cap, rows_ref.shape[1]), bf16)
    want = placement(counts, me, slots, slot_rows, total, 0)
    pg = dot_nn(want, rows_ref[:, :width]).astype(bf16)
    cot = dot_nn(want, rows_ref[:, width : 2 * width]).astype(bf16)
    pg_ref[...] = pg
    cot_ref[...] = cot
    spare = lanes - ff
    zeros = jnp.zeros((total, spare), f32)
    sums_ref[:, :ff] = dot_nn(pg, gate_w[...])
    sums_ref[:, ff:lanes] = dot_nn(want, rows_ref[:, 2 * width :])[:, :spare]
    sums_ref[:, lanes : lanes + ff] = dot_nn(pg, up_w[...])
    sums_ref[:, lanes + ff : 2 * lanes] = zeros
    sums_ref[:, 2 * lanes : 2 * lanes + ff] = dot_nt(cot, down_w[...])
    sums_ref[:, 2 * lanes + ff :] = zeros
    half = total // 2
    own_ref[...] = sums_ref[pl.ds(pl.multiple_of(core * half, half), half), :]
    send_ref[...] = sums_ref[pl.ds(pl.multiple_of((1 - core) * half, half), half), :].astype(bf16)


def add_kernel(own, got, out_ref, sum_ref):
    total = own[...] + got[...].astype(f32)
    sum_ref[...] = total
    out_ref[...] = total.astype(bf16)


def act_kernel(ff, lanes, model_width, own, got, out_ref):
    def part(i, size=ff, at=0):
        return own[:, i * lanes + at : i * lanes + at + size] + got[
            :, i * lanes + at : i * lanes + at + size
        ].astype(f32)

    scalars = part(0, lanes - ff, ff)
    kind = lax.broadcasted_iota(jnp.int32, scalars.shape, 1) % (2 * PARTS)
    logits = jnp.sum(jnp.where(kind < PARTS, scalars, 0.0), axis=1, keepdims=True)
    squares = jnp.sum(jnp.where(kind < PARTS, 0.0, scalars), axis=1, keepdims=True)
    gating = jax.nn.sigmoid(logits)
    inverse = lax.rsqrt(squares / model_width + epsilon)
    gate_raw, up_raw, dh_raw = part(0), part(1), part(2)
    gate_pre, up_pre = gate_raw * inverse, up_raw * inverse
    dhidden = dh_raw * gating
    sig = jax.nn.sigmoid(gate_pre)
    silu = gate_pre * sig
    hidden = (gating * silu * up_pre).astype(bf16)
    scaled = dhidden * inverse
    dgate = (scaled * up_pre * sig * (1.0 + gate_pre * (1.0 - sig))).astype(bf16)
    dup = (scaled * silu).astype(bf16)
    dlogit = (1.0 - gating) * jnp.sum(hidden.astype(f32) * dh_raw, axis=1, keepdims=True)
    inner = jnp.sum(dgate.astype(f32) * gate_raw + dup.astype(f32) * up_raw, axis=1, keepdims=True)
    inner = inner * inverse * inverse / model_width
    spare = lanes - ff
    zeros = jnp.zeros((own.shape[0], spare), bf16)
    out_ref[:, :ff] = hidden
    out_ref[:, ff:lanes] = in_lanes(terms(dlogit) + terms(inner), spare, 0).astype(bf16)
    out_ref[:, lanes : lanes + ff] = dgate
    out_ref[:, lanes + ff : 2 * lanes] = zeros
    out_ref[:, 2 * lanes : 2 * lanes + ff] = dup
    out_ref[:, 2 * lanes + ff :] = zeros


def second_kernel(slots, cap, slot_rows, lanes, counts, own, got, gate_w, up_w, down_w, *refs):
    outs = refs[:slots]
    hidden_ref, dgate_ref, dup_ref, act_ref, rows_ref = refs[slots:]
    me = lax.axis_index("dp")
    core = lax.axis_index("tensor") % 2
    width, ff = gate_w.shape
    half = own.shape[0]
    total = 2 * half
    act_ref[pl.ds(pl.multiple_of(core * half, half), half), :] = own[...]
    act_ref[pl.ds(pl.multiple_of((1 - core) * half, half), half), :] = got[...]
    hidden = act_ref[:, :ff]
    dgate = act_ref[:, lanes : lanes + ff]
    dup = act_ref[:, 2 * lanes : 2 * lanes + ff]
    hidden_ref[...] = hidden
    dgate_ref[...] = dgate
    dup_ref[...] = dup
    rows_ref[:, :width] = dot_nn(hidden, down_w[...]).astype(bf16)
    rows_ref[:, width : 2 * width] = (dot_nt(dgate, gate_w[...]) + dot_nt(dup, up_w[...])).astype(bf16)
    spare = lanes - ff
    rows_ref[:, 2 * width : 2 * width + spare] = act_ref[:, ff:lanes]
    rows_ref[:, 2 * width + spare :] = jnp.zeros((total, rows_ref.shape[1] - 2 * width - spare), bf16)
    want = placement(counts, me, slots, slot_rows, total, 1)
    slotted = dot_nn(want, rows_ref[...]).astype(bf16)
    for k in range(slots):
        outs[k][...] = slotted[k * slot_rows : k * slot_rows + cap]


def last_kernel(slots, cap, counts, chosen, *refs):
    blocks = refs[:slots]
    picked, load, mixed, cot, router, gain, updated_ref, grad_ref = refs[slots:]
    me = lax.axis_index("dp")
    mine = counts[0, me]
    tokens, width = cot.shape
    sums = blocks[0][...].astype(f32)
    for block in blocks[1:]:
        sums = sums + block[...].astype(f32)
    scalars = sums[:, 2 * width :]
    lane = lax.broadcasted_iota(jnp.int32, scalars.shape, 1)
    dlogit = jnp.sum(jnp.where(lane < PARTS, scalars, 0.0), axis=1, keepdims=True)
    inner = jnp.sum(jnp.where(lane < PARTS, 0.0, scalars), axis=1, keepdims=True)
    new_rows = (picked[...] + sums[:, :width]).astype(bf16)
    drows = (
        load[:, width : 2 * width].astype(f32)
        + sums[:, width : 2 * width] * gain[...].astype(f32)
        - picked[...] * inner
        + dlogit * router[...].astype(f32)
    ).astype(bf16)
    row = lax.broadcasted_iota(jnp.int32, (tokens, cap), 0)
    col = lax.broadcasted_iota(jnp.int32, (tokens, cap), 1)
    want = jnp.zeros((tokens, cap), f32)
    for k in range(cap):
        want = jnp.where((col == k) & (row == chosen[0, k]) & (k < mine), 1.0, want)
    is_chosen = jnp.sum(want, axis=1, keepdims=True) > 0.0
    want = want.astype(bf16)
    updated_ref[...] = jnp.where(is_chosen, dot_nn(want, new_rows), mixed[...].astype(f32)).astype(bf16)
    grad_ref[...] = jnp.where(is_chosen, dot_nn(want, drows), cot[...].astype(f32)).astype(bf16)


def fast(states, mix_weights, router, norm_gain, gate_weight, up_weight, down_weight, counts, chosen, cotangent):
    slots = lax.axis_size("dp")
    tensor = lax.axis_size("tensor")
    cap = chosen.shape[1]
    tokens, width = cotangent.shape
    ff = gate_weight.shape[1]
    model_width = width * tensor
    total = counts.shape[0] * counts.shape[1] * tokens // 8
    half = total // 2
    slot_rows = (cap + 15) // 16 * 16
    lanes = (ff + 2 * PARTS * tensor + 127) // 128 * 128
    router, gain = router.reshape(1, width), norm_gain.reshape(1, width)
    columns = 2 * width + 128

    def over_dp(x, k):
        return lax.ppermute(x, "dp", [(i, i ^ k) for i in range(slots)])

    def over_tensor(x, k):
        return lax.ppermute(x, "tensor", [(i, i ^ k) for i in range(tensor)])

    picked, load = call(
        functools.partial(pick_kernel, cap),
        (sds((cap, width), f32), sds((cap, columns), bf16)),
        [SMEM, SMEM, VMEM, VMEM, VMEM, VMEM],
    )(chosen, mix_weights, states, cotangent, router, gain)
    order = [k for k in (6, 7, 4, 5, 2, 3, 1) if k < slots]
    got = {k: over_dp(load, k) for k in order}
    mixed = jnp.tensordot(mix_weights, states.astype(f32), axes=1).astype(bf16)
    weights = (gate_weight, up_weight, down_weight)
    own, send, pg, cot = call(
        functools.partial(first_kernel, slots, cap, slot_rows, lanes),
        (sds((half, 3 * lanes), f32), sds((half, 3 * lanes), bf16), sds((total, width), bf16), sds((total, width), bf16)),
        [SMEM] + [VMEM] * (slots + 3),
        [pltpu.VMEM((slots * slot_rows, columns), bf16), pltpu.VMEM((total, 3 * lanes), f32)],
    )(counts, load, *[got[k] for k in range(1, slots)], *weights)
    send, own = call(
        add_kernel, (sds((half, 3 * lanes), bf16), sds((half, 3 * lanes), f32)), [VMEM] * 2
    )(own, over_tensor(send, 1))
    act = call(
        functools.partial(act_kernel, ff, lanes, model_width), sds((half, 3 * lanes), bf16), [VMEM] * 2
    )(own, over_tensor(send, 2))
    *blocks, hidden, dgate, dup = call(
        functools.partial(second_kernel, slots, cap, slot_rows, lanes),
        tuple([sds((cap, columns), bf16)] * slots + [sds((total, ff), bf16)] * 3),
        [SMEM] + [VMEM] * 5,
        [pltpu.VMEM((total, 3 * lanes), bf16), pltpu.VMEM((total, columns), bf16)],
    )(counts, act, over_tensor(act, 1), *weights)
    back = {k: over_dp(blocks[k], k) for k in order}
    grad_down = jnp.dot(hidden.T, cot, preferred_element_type=f32)
    grad_gate = jnp.dot(pg.T, dgate, preferred_element_type=f32)
    grad_up = jnp.dot(pg.T, dup, preferred_element_type=f32)
    updated, grad_input = call(
        functools.partial(last_kernel, slots, cap),
        (sds((tokens, width), bf16), sds((tokens, width), bf16)),
        [SMEM, SMEM] + [VMEM] * (slots + 6),
    )(counts, chosen, blocks[0], *[back[k] for k in range(1, slots)], picked, load, mixed, cotangent, router, gain)
    return updated, grad_input, grad_gate, grad_up, grad_down


def general(
    states,
    mix_weights,
    router,
    norm_gain,
    gate_weight,
    up_weight,
    down_weight,
    counts,
    chosen,
    cotangent,
):
    width_here = cotangent.shape[1]
    my_rank = lax.axis_index("dp")
    model_width = width_here * lax.axis_size("tensor")
    mixed = jnp.tensordot(mix_weights, states.astype(jnp.float32), axes=1)
    flat_counts = counts.reshape(-1)
    my_count = flat_counts[my_rank]
    positions = chosen[0]
    capacity = positions.shape[0]
    slot_ids = jnp.arange(capacity, dtype=jnp.int32)
    is_valid = slot_ids < my_count
    valid = is_valid.astype(jnp.float32)[:, None]
    picked = mixed[positions]
    router_float = router.astype(jnp.float32)
    gain_float = norm_gain.astype(jnp.float32)
    logit_part = jnp.sum(picked * router_float, axis=1)
    square_part = jnp.sum(picked * picked, axis=1)
    logits, squares = lax.psum((logit_part, square_part), "tensor")
    gating = jax.nn.sigmoid(logits)
    inverse = lax.rsqrt(squares / model_width + epsilon)
    normed = (picked * inverse[:, None] * gain_float * valid).astype(jnp.bfloat16)
    gathered = lax.all_gather(normed, "dp", axis=0, tiled=True)
    gate_part = jnp.dot(gathered, gate_weight, preferred_element_type=jnp.float32)
    up_part = jnp.dot(gathered, up_weight, preferred_element_type=jnp.float32)
    gate_pre, up_pre = lax.psum((gate_part, up_part), "tensor")
    hidden = (jax.nn.silu(gate_pre) * up_pre).astype(jnp.bfloat16)
    update_work = lax.psum_scatter(
        jnp.dot(hidden, down_weight, preferred_element_type=jnp.float32),
        "dp",
        scatter_dimension=0,
        tiled=True,
    ).astype(jnp.bfloat16)
    update_float = update_work.astype(jnp.float32) * valid
    new_rows = picked + gating[:, None] * update_float
    result = mixed.at[positions].set(new_rows).astype(jnp.bfloat16)
    cot_rows = cotangent[positions].astype(jnp.float32)
    dupdate = (gating[:, None] * cot_rows * valid).astype(jnp.bfloat16)
    dlogit_part = jnp.sum(cot_rows * update_float, axis=1)
    dgathered = lax.all_gather(dupdate, "dp", axis=0, tiled=True)
    dhidden_part = jnp.dot(dgathered, down_weight.T, preferred_element_type=jnp.float32)
    dhidden = lax.psum(dhidden_part, "tensor")
    sigmoid_pre = jax.nn.sigmoid(gate_pre)
    dgate_pre = (dhidden * up_pre * sigmoid_pre * (1.0 + gate_pre * (1.0 - sigmoid_pre))).astype(
        jnp.bfloat16
    )
    dup_pre = (dhidden * gate_pre * sigmoid_pre).astype(jnp.bfloat16)
    grad_down = jnp.dot(hidden.T, dgathered, preferred_element_type=jnp.float32)
    grad_gate = jnp.dot(gathered.T, dgate_pre, preferred_element_type=jnp.float32)
    grad_up = jnp.dot(gathered.T, dup_pre, preferred_element_type=jnp.float32)
    first_term = jnp.dot(dgate_pre, gate_weight.T, preferred_element_type=jnp.float32)
    dnormed_work = lax.psum_scatter(
        first_term + jnp.dot(dup_pre, up_weight.T, preferred_element_type=jnp.float32),
        "dp",
        scatter_dimension=0,
        tiled=True,
    )
    scaled = dnormed_work * gain_float * valid
    inner_part = jnp.sum(scaled * picked, axis=1)
    dlogit_sum, inner_sum = lax.psum((dlogit_part, inner_part), "tensor")
    dlogit = dlogit_sum * gating * (1.0 - gating)
    drows = (
        cot_rows
        + inverse[:, None] * scaled
        - picked * (inverse**3 * inner_sum / model_width)[:, None]
        + valid * dlogit[:, None] * router_float
    )
    grad_input = cotangent.astype(jnp.float32).at[positions].set(drows).astype(jnp.bfloat16)
    return (result, grad_input, grad_gate, grad_up, grad_down)


def solution(mesh):
    return jax.shard_map(
        fast if (mesh.shape["dp"], mesh.shape["tensor"]) == (8, 4) else general,
        mesh=mesh,
        in_specs=(
            P(None, "dp", "tensor"),
            P(),
            P("tensor"),
            P("tensor"),
            P("tensor", "dp"),
            P("tensor", "dp"),
            P("dp", "tensor"),
            P(),
            P("dp", None),
            P("dp", "tensor"),
        ),
        out_specs=(
            P("dp", "tensor"),
            P("dp", "tensor"),
            P("tensor", "dp"),
            P("tensor", "dp"),
            P("dp", "tensor"),
        ),
        check_vma=False,
    )
```

```python
import functools
import jax
import jax.numpy as jnp
from jax import lax
from jax.experimental import pallas as pl
from jax.experimental.pallas import tpu as pltpu
from jax.sharding import PartitionSpec as P


epsilon = 1e-05
f32, bf16 = jnp.float32, jnp.bfloat16
SMEM = pl.BlockSpec(memory_space=pltpu.SMEM)
VMEM = pl.BlockSpec(memory_space=pltpu.VMEM)
PARTS = 3


def call(kernel, out, ins, scratch=(), flops=0, nbytes=0, vmem=32 << 20):
    return pl.pallas_call(
        kernel,
        out_shape=out,
        in_specs=ins,
        out_specs=jax.tree.map(lambda _: VMEM, out),
        scratch_shapes=list(scratch),
        cost_estimate=pl.CostEstimate(flops=flops, bytes_accessed=nbytes, transcendentals=0),
        compiler_params=pltpu.CompilerParams(vmem_limit_bytes=vmem),
    )


def sds(shape, dtype):
    return jax.ShapeDtypeStruct(shape, dtype)


def terms(value):
    out, rest = [], value
    for _ in range(PARTS):
        term = rest.astype(bf16).astype(f32)
        out.append(term)
        rest = rest - term
    return out


def in_lanes(values, width, first):
    rows = values[0].shape[0]
    lane = lax.broadcasted_iota(jnp.int32, (rows, width), 1)
    total = jnp.zeros((rows, width), f32)
    for i, value in enumerate(values):
        total = jnp.where(lane == first + i, value, total)
    return total


def dot_nt(a, b):
    return lax.dot_general(a, b, (((1,), (1,)), ((), ())), preferred_element_type=f32)


def dot_nn(a, b):
    return jnp.dot(a, b, preferred_element_type=f32)


def placement(counts_ref, me, slots, slot_rows, total, packed_axis):
    shape = (total, slots * slot_rows) if packed_axis == 0 else (slots * slot_rows, total)
    packed = lax.broadcasted_iota(jnp.int32, shape, packed_axis)
    slotted = lax.broadcasted_iota(jnp.int32, shape, 1 - packed_axis)
    hit, at = packed < 0, 0
    for k in range(slots):
        here = counts_ref[0, me ^ k]
        row = slotted - k * slot_rows
        hit = hit | ((row >= 0) & (row < here) & (packed == row + at))
        at = at + here
    return jnp.where(hit, 1.0, 0.0).astype(bf16)


def fetch(pairs, sem):
    copies = [pltpu.make_async_copy(src, dst, sem.at[i]) for i, (src, dst) in enumerate(pairs)]
    for copy in copies:
        copy.start()
    return copies


def pick_kernel(cap, chosen, mixw, states, cot, router, gain, picked_ref, load_ref, *scratch):
    *places, sem = scratch
    for copy in fetch(list(zip((chosen, mixw, states, cot, router, gain), places)), sem):
        copy.wait()
    chosen, mixw, states, cot, router, gain = places
    tokens, width = cot.shape
    row = lax.broadcasted_iota(jnp.int32, (cap, tokens), 0)
    col = lax.broadcasted_iota(jnp.int32, (cap, tokens), 1)
    want = jnp.zeros((cap, tokens), f32)
    for k in range(cap):
        want = jnp.where((row == k) & (col == chosen[0, k]), 1.0, want)
    want = want.astype(bf16)
    picked = mixw[0] * dot_nn(want, states[0])
    for j in range(1, states.shape[0]):
        picked = picked + mixw[j] * dot_nn(want, states[j])
    picked_ref[...] = picked
    load_ref[:, :width] = (picked * gain[...].astype(f32).reshape(1, width)).astype(bf16)
    load_ref[:, width : 2 * width] = dot_nn(want, cot[...]).astype(bf16)
    logit = jnp.sum(picked * router[...].astype(f32).reshape(1, width), axis=1, keepdims=True)
    square = jnp.sum(picked * picked, axis=1, keepdims=True)
    first = 2 * PARTS * lax.axis_index("tensor")
    load_ref[:, 2 * width :] = in_lanes(terms(logit) + terms(square), 128, first).astype(bf16)


def weights_kernel(slots, slot_rows, total, after, *refs):
    *pairs, pack_ref, unpack_ref, counts, sem = refs
    half = len(pairs) // 2
    copies = fetch(list(zip(pairs[: half + 1], [counts] + pairs[half + 1 :])), sem)
    copies[0].wait()
    me = lax.axis_index("dp")
    pack_ref[...] = placement(counts, me, slots, slot_rows, total, 0)
    unpack_ref[...] = placement(counts, me, slots, slot_rows, total, 1)
    for copy in copies[1:]:
        copy.wait()


def prep_kernel(after, counts, chosen, mixw, states, cot, *refs):
    mixed_ref, cot_ref, want_ref, *places, sem = refs
    for copy in fetch(list(zip((counts, chosen, mixw, states, cot), places)), sem):
        copy.wait()
    counts, chosen, mixw, states, cot = places
    me = lax.axis_index("dp")
    mine = counts[0, me]
    tokens, cap = want_ref.shape
    row = lax.broadcasted_iota(jnp.int32, (tokens, cap), 0)
    col = lax.broadcasted_iota(jnp.int32, (tokens, cap), 1)
    want = jnp.zeros((tokens, cap), f32)
    for k in range(cap):
        want = jnp.where((col == k) & (row == chosen[0, k]) & (k < mine), 1.0, want)
    want_ref[...] = want.astype(bf16)
    keep = jnp.sum(want, axis=1, keepdims=True) == 0.0
    mixed = mixw[0] * states[0].astype(f32)
    for j in range(1, states.shape[0]):
        mixed = mixed + mixw[j] * states[j].astype(f32)
    mixed_ref[...] = jnp.where(keep, mixed, 0.0).astype(bf16)
    cot_ref[...] = jnp.where(keep, cot[...].astype(f32), 0.0).astype(bf16)


def first_kernel(slots, cap, slot_rows, lanes, want, *refs):
    blocks = refs[:slots]
    gate_w, up_w, down_w, own_ref, send_ref, pg_ref, cot_ref, rows_ref, sums_ref, mine_ref, sem = refs[slots:]
    copies = fetch([(blocks[0], mine_ref)], sem)
    core = lax.axis_index("tensor") % 2
    ff, width = gate_w.shape
    total = pg_ref.shape[0]
    for k in reversed(range(slots)):
        if k == 0:
            copies[0].wait()
        rows_ref[k * slot_rows : k * slot_rows + cap, :] = (blocks[k] if k else mine_ref)[...]
        rows_ref[k * slot_rows + cap : (k + 1) * slot_rows, :] = jnp.zeros((slot_rows - cap, rows_ref.shape[1]), bf16)
    pg = dot_nn(want[...], rows_ref[:, :width]).astype(bf16)
    cot = dot_nn(want[...], rows_ref[:, width : 2 * width]).astype(bf16)
    pg_ref[...] = pg
    cot_ref[...] = cot
    spare = lanes - ff
    zeros = jnp.zeros((total, spare), f32)
    sums_ref[:, :ff] = dot_nt(pg, gate_w[...])
    sums_ref[:, ff:lanes] = dot_nn(want[...], rows_ref[:, 2 * width :])[:, :spare]
    sums_ref[:, lanes : lanes + ff] = dot_nt(pg, up_w[...])
    sums_ref[:, lanes + ff : 2 * lanes] = zeros
    sums_ref[:, 2 * lanes : 2 * lanes + ff] = dot_nt(cot, down_w[...])
    sums_ref[:, 2 * lanes + ff :] = zeros
    half = total // 2
    own_ref[...] = sums_ref[pl.ds(pl.multiple_of(core * half, half), half), :]
    send_ref[...] = sums_ref[pl.ds(pl.multiple_of((1 - core) * half, half), half), :].astype(bf16)


def add_kernel(own, got, out_ref, sum_ref):
    total = own[...] + got[...].astype(f32)
    sum_ref[...] = total
    out_ref[...] = total.astype(bf16)


def act_kernel(ff, lanes, model_width, own, got, out_ref):
    def part(i, size=ff, at=0):
        return own[:, i * lanes + at : i * lanes + at + size] + got[
            :, i * lanes + at : i * lanes + at + size
        ].astype(f32)

    scalars = part(0, lanes - ff, ff)
    kind = lax.broadcasted_iota(jnp.int32, scalars.shape, 1) % (2 * PARTS)
    logits = jnp.sum(jnp.where(kind < PARTS, scalars, 0.0), axis=1, keepdims=True)
    squares = jnp.sum(jnp.where(kind < PARTS, 0.0, scalars), axis=1, keepdims=True)
    gating = jax.nn.sigmoid(logits)
    inverse = lax.rsqrt(squares / model_width + epsilon)
    gate_raw, up_raw, dh_raw = part(0), part(1), part(2)
    gate_pre, up_pre = gate_raw * inverse, up_raw * inverse
    dhidden = dh_raw * gating
    sig = jax.nn.sigmoid(gate_pre)
    silu = gate_pre * sig
    hidden = (gating * silu * up_pre).astype(bf16)
    scaled = dhidden * inverse
    dgate = (scaled * up_pre * sig * (1.0 + gate_pre * (1.0 - sig))).astype(bf16)
    dup = (scaled * silu).astype(bf16)
    dlogit = (1.0 - gating) * jnp.sum(hidden.astype(f32) * dh_raw, axis=1, keepdims=True)
    inner = jnp.sum(dgate.astype(f32) * gate_raw + dup.astype(f32) * up_raw, axis=1, keepdims=True)
    inner = inner * inverse * inverse / model_width
    spare = lanes - ff
    zeros = jnp.zeros((own.shape[0], spare), bf16)
    first = 2 * PARTS * (lax.axis_index("dp") % 4)
    out_ref[:, :ff] = hidden
    out_ref[:, ff:lanes] = in_lanes(terms(dlogit) + terms(inner), spare, first).astype(bf16)
    out_ref[:, lanes : lanes + ff] = dgate
    out_ref[:, lanes + ff : 2 * lanes] = zeros
    out_ref[:, 2 * lanes : 2 * lanes + ff] = dup
    out_ref[:, 2 * lanes + ff :] = zeros


def second_kernel(slots, cap, slot_rows, lanes, want, own, got, gate_w, up_w, down_w, *refs):
    outs = refs[:slots]
    hidden_ref, dgate_ref, dup_ref, act_ref, rows_ref = refs[slots:]
    core = lax.axis_index("tensor") % 2
    ff, width = gate_w.shape
    half = own.shape[0]
    total = 2 * half
    act_ref[pl.ds(pl.multiple_of(core * half, half), half), :] = own[...]
    act_ref[pl.ds(pl.multiple_of((1 - core) * half, half), half), :] = got[...]
    hidden = act_ref[:, :ff]
    dgate = act_ref[:, lanes : lanes + ff]
    dup = act_ref[:, 2 * lanes : 2 * lanes + ff]
    hidden_ref[...] = hidden
    dgate_ref[...] = dgate
    dup_ref[...] = dup
    rows_ref[:, :width] = dot_nn(hidden, down_w[...]).astype(bf16)
    rows_ref[:, width : 2 * width] = (dot_nn(dgate, gate_w[...]) + dot_nn(dup, up_w[...])).astype(bf16)
    spare = lanes - ff
    rows_ref[:, 2 * width : 2 * width + spare] = act_ref[:, ff:lanes]
    rows_ref[:, 2 * width + spare :] = jnp.zeros((total, rows_ref.shape[1] - 2 * width - spare), bf16)
    slotted = dot_nn(want[...], rows_ref[...]).astype(bf16)
    for k in range(slots):
        outs[k][...] = slotted[k * slot_rows : k * slot_rows + cap]


def last_kernel(want, picked, load, mixed, cot, router, gain, *refs):
    *blocks, updated_ref, grad_ref = refs
    _, width = cot.shape
    sums = blocks[0][...].astype(f32)
    for block in blocks[1:]:
        sums = sums + block[...].astype(f32)
    scalars = sums[:, 2 * width :]
    kind = lax.broadcasted_iota(jnp.int32, scalars.shape, 1) % (2 * PARTS)
    dlogit = jnp.sum(jnp.where(kind < PARTS, scalars, 0.0), axis=1, keepdims=True)
    inner = jnp.sum(jnp.where(kind < PARTS, 0.0, scalars), axis=1, keepdims=True)
    new_rows = (picked[...] + sums[:, :width]).astype(bf16)
    drows = (
        load[:, width : 2 * width].astype(f32)
        + sums[:, width : 2 * width] * gain[...].astype(f32)
        - picked[...] * inner
        + dlogit * router[...].astype(f32)
    ).astype(bf16)
    updated_ref[...] = (mixed[...].astype(f32) + dot_nn(want[...], new_rows)).astype(bf16)
    grad_ref[...] = (cot[...].astype(f32) + dot_nn(want[...], drows)).astype(bf16)


def fast(states, mix_weights, router, norm_gain, gate_weight, up_weight, down_weight, counts, chosen, cotangent):
    slots = lax.axis_size("dp")
    tensor = lax.axis_size("tensor")
    cap = chosen.shape[1]
    tokens, width = cotangent.shape
    ff = gate_weight.shape[1]
    model_width = width * tensor
    total = counts.shape[0] * counts.shape[1] * tokens // 8
    half = total // 2
    slot_rows = (cap + 15) // 16 * 16
    lanes = (ff + 2 * PARTS * tensor + 127) // 128 * 128
    columns = 2 * width + 128
    anywhere = pl.BlockSpec(memory_space=pltpu.HBM)
    block = sds((cap, columns), bf16)

    def over_dp(x, k):
        return lax.ppermute(x, "dp", [(i, i ^ k) for i in range(slots)])

    def over_tensor(x, k):
        return lax.ppermute(x, "tensor", [(i, i ^ k) for i in range(tensor)])

    def copy_of(x, space=pltpu.VMEM):
        return space(x.shape, x.dtype)

    sem = pltpu.SemaphoreType.DMA((8,))
    picked, load = call(
        functools.partial(pick_kernel, cap),
        (sds((cap, width), f32), block),
        [anywhere] * 6,
        [copy_of(chosen, pltpu.SMEM), copy_of(mix_weights, pltpu.SMEM)]
        + [copy_of(x) for x in (states, cotangent, router, norm_gain)]
        + [sem],
        vmem=65_000_000,
    )(chosen, mix_weights, states, cotangent, router, norm_gain)
    gate_t, up_t = gate_weight.T, up_weight.T
    blocks = {0: load}
    for step in (4, 2, 1):
        for k in list(blocks):
            blocks[k ^ step] = over_dp(blocks[k], step)
    weight = sds((ff, width), bf16)
    gate_v, up_v, down_v, pack, unpack = call(
        functools.partial(weights_kernel, slots, slot_rows, total),
        (weight,) * 3 + (sds((total, slots * slot_rows), bf16), sds((slots * slot_rows, total), bf16)),
        [pl.BlockSpec(memory_space=pl.ANY)] + [anywhere] * 4,
        [copy_of(counts, pltpu.SMEM), sem],
        nbytes=13 << 20,
        vmem=48_000_000,
    )(load, counts, gate_t, up_t, down_weight)
    weights = (gate_v, up_v, down_v)
    own, send, pg, cot = call(
        functools.partial(first_kernel, slots, cap, slot_rows, lanes),
        (sds((half, 3 * lanes), f32), sds((half, 3 * lanes), bf16), sds((total, width), bf16), sds((total, width), bf16)),
        [VMEM, pl.BlockSpec(memory_space=pl.ANY)] + [VMEM] * (slots + 2),
        [pltpu.VMEM((slots * slot_rows, columns), bf16), pltpu.VMEM((total, 3 * lanes), f32), copy_of(load), sem],
    )(pack, *[blocks[k] for k in range(slots)], *weights)
    send, own = call(
        add_kernel, (sds((half, 3 * lanes), bf16), sds((half, 3 * lanes), f32)), [VMEM] * 2
    )(own, over_tensor(send, 1))
    mixed, cot_kept, want = call(
        prep_kernel,
        (sds((tokens, width), bf16), sds((tokens, width), bf16), sds((tokens, cap), bf16)),
        [VMEM] + [anywhere] * 5,
        [copy_of(x, pltpu.SMEM) for x in (counts, chosen, mix_weights)] + [copy_of(states), copy_of(cotangent), sem],
        nbytes=3 << 20,
    )(send, counts, chosen, mix_weights, states, cotangent)
    act = call(
        functools.partial(act_kernel, ff, lanes, model_width), sds((half, 3 * lanes), bf16), [VMEM] * 2
    )(own, over_tensor(send, 2))
    *blocks, hidden, dgate, dup = call(
        functools.partial(second_kernel, slots, cap, slot_rows, lanes),
        tuple([block] * slots + [sds((total, ff), bf16)] * 3),
        [VMEM] * 6,
        [pltpu.VMEM((total, 3 * lanes), bf16), pltpu.VMEM((total, columns), bf16)],
    )(unpack, act, over_tensor(act, 1), *weights)

    def moved(value, step):
        return over_dp(value, step).astype(f32)

    def total_of(k, *more):
        return sum(more, blocks[k].astype(f32) + moved(blocks[k ^ 1], 1)).astype(bf16)

    sum_4 = total_of(4, moved(total_of(6), 2))
    back = [over_dp(blocks[1], 1), over_dp(total_of(2), 2), over_dp(sum_4, 4)]
    dot_tn = functools.partial(lax.dot_general, dimension_numbers=(((0,), (0,)), ((), ())), preferred_element_type=f32)
    grad_down = dot_tn(hidden, cot)
    grad_gate = dot_tn(dgate, pg).T
    grad_up = dot_tn(dup, pg).T
    updated, grad_input = call(
        last_kernel, (sds((tokens, width), bf16), sds((tokens, width), bf16)), [VMEM] * 11
    )(want, picked, load, mixed, cot_kept, router.reshape(1, width), norm_gain.reshape(1, width), blocks[0], *back)
    return updated, grad_input, grad_gate, grad_up, grad_down


def general(
    states,
    mix_weights,
    router,
    norm_gain,
    gate_weight,
    up_weight,
    down_weight,
    counts,
    chosen,
    cotangent,
):
    width_here = cotangent.shape[1]
    my_rank = lax.axis_index("dp")
    model_width = width_here * lax.axis_size("tensor")
    mixed = jnp.tensordot(mix_weights, states.astype(jnp.float32), axes=1)
    flat_counts = counts.reshape(-1)
    my_count = flat_counts[my_rank]
    positions = chosen[0]
    capacity = positions.shape[0]
    slot_ids = jnp.arange(capacity, dtype=jnp.int32)
    is_valid = slot_ids < my_count
    valid = is_valid.astype(jnp.float32)[:, None]
    picked = mixed[positions]
    router_float = router.astype(jnp.float32)
    gain_float = norm_gain.astype(jnp.float32)
    logit_part = jnp.sum(picked * router_float, axis=1)
    square_part = jnp.sum(picked * picked, axis=1)
    logits, squares = lax.psum((logit_part, square_part), "tensor")
    gating = jax.nn.sigmoid(logits)
    inverse = lax.rsqrt(squares / model_width + epsilon)
    normed = (picked * inverse[:, None] * gain_float * valid).astype(jnp.bfloat16)
    gathered = lax.all_gather(normed, "dp", axis=0, tiled=True)
    gate_part = jnp.dot(gathered, gate_weight, preferred_element_type=jnp.float32)
    up_part = jnp.dot(gathered, up_weight, preferred_element_type=jnp.float32)
    gate_pre, up_pre = lax.psum((gate_part, up_part), "tensor")
    hidden = (jax.nn.silu(gate_pre) * up_pre).astype(jnp.bfloat16)
    update_work = lax.psum_scatter(
        jnp.dot(hidden, down_weight, preferred_element_type=jnp.float32),
        "dp",
        scatter_dimension=0,
        tiled=True,
    ).astype(jnp.bfloat16)
    update_float = update_work.astype(jnp.float32) * valid
    new_rows = picked + gating[:, None] * update_float
    result = mixed.at[positions].set(new_rows).astype(jnp.bfloat16)
    cot_rows = cotangent[positions].astype(jnp.float32)
    dupdate = (gating[:, None] * cot_rows * valid).astype(jnp.bfloat16)
    dlogit_part = jnp.sum(cot_rows * update_float, axis=1)
    dgathered = lax.all_gather(dupdate, "dp", axis=0, tiled=True)
    dhidden_part = jnp.dot(dgathered, down_weight.T, preferred_element_type=jnp.float32)
    dhidden = lax.psum(dhidden_part, "tensor")
    sigmoid_pre = jax.nn.sigmoid(gate_pre)
    dgate_pre = (dhidden * up_pre * sigmoid_pre * (1.0 + gate_pre * (1.0 - sigmoid_pre))).astype(
        jnp.bfloat16
    )
    dup_pre = (dhidden * gate_pre * sigmoid_pre).astype(jnp.bfloat16)
    grad_down = jnp.dot(hidden.T, dgathered, preferred_element_type=jnp.float32)
    grad_gate = jnp.dot(gathered.T, dgate_pre, preferred_element_type=jnp.float32)
    grad_up = jnp.dot(gathered.T, dup_pre, preferred_element_type=jnp.float32)
    first_term = jnp.dot(dgate_pre, gate_weight.T, preferred_element_type=jnp.float32)
    dnormed_work = lax.psum_scatter(
        first_term + jnp.dot(dup_pre, up_weight.T, preferred_element_type=jnp.float32),
        "dp",
        scatter_dimension=0,
        tiled=True,
    )
    scaled = dnormed_work * gain_float * valid
    inner_part = jnp.sum(scaled * picked, axis=1)
    dlogit_sum, inner_sum = lax.psum((dlogit_part, inner_part), "tensor")
    dlogit = dlogit_sum * gating * (1.0 - gating)
    drows = (
        cot_rows
        + inverse[:, None] * scaled
        - picked * (inverse**3 * inner_sum / model_width)[:, None]
        + valid * dlogit[:, None] * router_float
    )
    grad_input = cotangent.astype(jnp.float32).at[positions].set(drows).astype(jnp.bfloat16)
    return (result, grad_input, grad_gate, grad_up, grad_down)


def solution(mesh):
    small = (mesh.shape["dp"], mesh.shape["tensor"]) == (8, 4)
    return jax.shard_map(
        fast if small else general,
        mesh=mesh,
        in_specs=(
            P(None, "dp", "tensor"),
            P(),
            P("tensor"),
            P("tensor"),
            P("tensor", "dp"),
            P("tensor", "dp"),
            P("dp", "tensor"),
            P(),
            P("dp", None),
            P("dp", "tensor"),
        ),
        out_specs=(
            P("dp", "tensor"),
            P("dp", "tensor"),
            P("tensor", "dp"),
            P("tensor", "dp"),
            P("dp", "tensor"),
        ),
        check_vma=False,
    )
```

```python
import functools
import jax
import jax.numpy as jnp
from jax import lax
from jax.experimental import pallas as pl
from jax.experimental.pallas import tpu as pltpu
from jax.sharding import PartitionSpec as P


epsilon = 1e-05
f32, bf16 = jnp.float32, jnp.bfloat16
SMEM = pl.BlockSpec(memory_space=pltpu.SMEM)
VMEM = pl.BlockSpec(memory_space=pltpu.VMEM)
PARTS = 3


def call(kernel, out, ins, scratch=(), flops=0, nbytes=0, vmem=32 << 20):
    return pl.pallas_call(
        kernel,
        out_shape=out,
        in_specs=ins,
        out_specs=jax.tree.map(lambda _: VMEM, out),
        scratch_shapes=list(scratch),
        cost_estimate=pl.CostEstimate(flops=flops, bytes_accessed=nbytes, transcendentals=0),
        compiler_params=pltpu.CompilerParams(vmem_limit_bytes=vmem),
    )


def sds(shape, dtype):
    return jax.ShapeDtypeStruct(shape, dtype)


def terms(value):
    out, rest = [], value
    for _ in range(PARTS):
        term = rest.astype(bf16).astype(f32)
        out.append(term)
        rest = rest - term
    return out


def in_lanes(values, width, first):
    rows = values[0].shape[0]
    lane = lax.broadcasted_iota(jnp.int32, (rows, width), 1)
    total = jnp.zeros((rows, width), f32)
    for i, value in enumerate(values):
        total = jnp.where(lane == first + i, value, total)
    return total


def dot_nt(a, b):
    return lax.dot_general(a, b, (((1,), (1,)), ((), ())), preferred_element_type=f32)


def dot_nn(a, b):
    return jnp.dot(a, b, preferred_element_type=f32)


def fetch(pairs, sem):
    copies = [pltpu.make_async_copy(src, dst, sem.at[i]) for i, (src, dst) in enumerate(pairs)]
    for copy in copies:
        copy.start()
    return copies


def pick_kernel(cap, counts, chosen, mixw, states, cot, router, gain, picked_ref, load_ref, *scratch):
    *places, sem = scratch
    for copy in fetch(list(zip((counts, chosen, mixw, states, cot, router, gain), places)), sem):
        copy.wait()
    counts, chosen, mixw, states, cot, router, gain = places
    mine = counts[0, lax.axis_index("dp")]
    tokens, width = cot.shape
    row = lax.broadcasted_iota(jnp.int32, (cap, tokens), 0)
    col = lax.broadcasted_iota(jnp.int32, (cap, tokens), 1)
    want = jnp.zeros((cap, tokens), f32)
    for k in range(cap):
        want = jnp.where((row == k) & (col == chosen[0, k]) & (k < mine), 1.0, want)
    want = want.astype(bf16)
    picked = mixw[0] * dot_nn(want, states[0])
    for j in range(1, states.shape[0]):
        picked = picked + mixw[j] * dot_nn(want, states[j])
    picked_ref[...] = picked
    load_ref[:, :width] = (picked * gain[...].astype(f32).reshape(1, width)).astype(bf16)
    load_ref[:, width : 2 * width] = dot_nn(want, cot[...]).astype(bf16)
    logit = jnp.sum(picked * router[...].astype(f32).reshape(1, width), axis=1, keepdims=True)
    square = jnp.sum(picked * picked, axis=1, keepdims=True)
    first = 2 * PARTS * lax.axis_index("tensor")
    load_ref[:, 2 * width :] = in_lanes(terms(logit) + terms(square), 128, first).astype(bf16)


def weights_kernel(after, *refs):
    *pairs, sem = refs
    half = len(pairs) // 2
    for copy in fetch(list(zip(pairs[:half], pairs[half:])), sem):
        copy.wait()


def prep_kernel(after, counts, chosen, mixw, states, cot, *refs):
    mixed_ref, cot_ref, want_ref, *places, sem = refs
    for copy in fetch(list(zip((counts, chosen, mixw, states, cot), places)), sem):
        copy.wait()
    counts, chosen, mixw, states, cot = places
    me = lax.axis_index("dp")
    mine = counts[0, me]
    tokens, cap = want_ref.shape
    row = lax.broadcasted_iota(jnp.int32, (tokens, cap), 0)
    col = lax.broadcasted_iota(jnp.int32, (tokens, cap), 1)
    want = jnp.zeros((tokens, cap), f32)
    for k in range(cap):
        want = jnp.where((col == k) & (row == chosen[0, k]) & (k < mine), 1.0, want)
    want_ref[...] = want.astype(bf16)
    keep = jnp.sum(want, axis=1, keepdims=True) == 0.0
    mixed = mixw[0] * states[0].astype(f32)
    for j in range(1, states.shape[0]):
        mixed = mixed + mixw[j] * states[j].astype(f32)
    mixed_ref[...] = jnp.where(keep, mixed, 0.0).astype(bf16)
    cot_ref[...] = jnp.where(keep, cot[...].astype(f32), 0.0).astype(bf16)


def first_kernel(slots, lanes, *refs):
    blocks, (gate_w, up_w, down_w, own_ref, send_ref, rows_ref, sums_ref) = refs[:slots], refs[slots : slots + 7]
    if len(refs) > slots + 7:
        mine_ref, sem = refs[slots + 7 :]
        (copy,) = fetch([(blocks[0], mine_ref)], sem)
        copy.wait()
        blocks = (mine_ref,) + blocks[1:]
    core = lax.axis_index("tensor") % 2
    ff, width = gate_w.shape
    rows = jnp.concatenate([block[...].astype(f32) for block in blocks], axis=0)
    spare = lanes - ff
    zeros = jnp.zeros((rows.shape[0], spare), f32)
    sums_ref[:, ff:lanes] = rows[:, 2 * width : 2 * width + spare]
    rows_ref[...] = rows[:, : 2 * width].astype(bf16)
    pg = rows_ref[:, :width]
    sums_ref[:, :ff] = dot_nt(pg, gate_w[...])
    sums_ref[:, lanes : lanes + ff] = dot_nt(pg, up_w[...])
    sums_ref[:, lanes + ff : 2 * lanes] = zeros
    sums_ref[:, 2 * lanes : 2 * lanes + ff] = dot_nt(rows_ref[:, width:], down_w[...])
    sums_ref[:, 2 * lanes + ff :] = zeros
    half = own_ref.shape[0]
    own_ref[...] = sums_ref[pl.ds(pl.multiple_of(core * half, 8), half), :]
    send_ref[...] = sums_ref[pl.ds(pl.multiple_of((1 - core) * half, 8), half), :].astype(bf16)


def add_kernel(own, got, out_ref, sum_ref):
    total = own[...] + got[...].astype(f32)
    sum_ref[...] = total
    out_ref[...] = total.astype(bf16)


def act_kernel(ff, lanes, model_width, own, got, out_ref):
    def part(i, size=ff, at=0):
        return own[:, i * lanes + at : i * lanes + at + size] + got[
            :, i * lanes + at : i * lanes + at + size
        ].astype(f32)

    scalars = part(0, lanes - ff, ff)
    kind = lax.broadcasted_iota(jnp.int32, scalars.shape, 1) % (2 * PARTS)
    logits = jnp.sum(jnp.where(kind < PARTS, scalars, 0.0), axis=1, keepdims=True)
    squares = jnp.sum(jnp.where(kind < PARTS, 0.0, scalars), axis=1, keepdims=True)
    gating = jax.nn.sigmoid(logits)
    inverse = lax.rsqrt(squares / model_width + epsilon)
    gate_raw, up_raw, dh_raw = part(0), part(1), part(2)
    gate_pre, up_pre = gate_raw * inverse, up_raw * inverse
    dhidden = dh_raw * gating
    sig = jax.nn.sigmoid(gate_pre)
    silu = gate_pre * sig
    hidden = (gating * silu * up_pre).astype(bf16)
    scaled = dhidden * inverse
    dgate = (scaled * up_pre * sig * (1.0 + gate_pre * (1.0 - sig))).astype(bf16)
    dup = (scaled * silu).astype(bf16)
    dlogit = (1.0 - gating) * jnp.sum(hidden.astype(f32) * dh_raw, axis=1, keepdims=True)
    inner = jnp.sum(dgate.astype(f32) * gate_raw + dup.astype(f32) * up_raw, axis=1, keepdims=True)
    inner = inner * inverse * inverse / model_width
    spare = lanes - ff
    zeros = jnp.zeros((own.shape[0], spare), bf16)
    first = 2 * PARTS * (lax.axis_index("dp") % 4)
    out_ref[:, :ff] = hidden
    out_ref[:, ff:lanes] = in_lanes(terms(dlogit) + terms(inner), spare, first).astype(bf16)
    out_ref[:, lanes : lanes + ff] = dgate
    out_ref[:, lanes + ff : 2 * lanes] = zeros
    out_ref[:, 2 * lanes : 2 * lanes + ff] = dup
    out_ref[:, 2 * lanes + ff :] = zeros


def second_kernel(slots, lanes, own, got, gate_w, up_w, down_w, *refs):
    outs, (act_ref,) = refs[:slots], refs[slots:]
    core = lax.axis_index("tensor") % 2
    ff, width = gate_w.shape
    cap = outs[0].shape[0]
    mine, other = own[...].astype(f32), got[...].astype(f32)
    order = (jnp.where(core == 0, mine, other), jnp.where(core == 0, other, mine))
    act_ref[...] = jnp.concatenate(order, axis=0).astype(bf16)
    spare = lanes - ff
    update = dot_nn(act_ref[:, :ff], down_w[...])
    dnormed = dot_nn(act_ref[:, lanes : lanes + ff], gate_w[...])
    dnormed = dnormed + dot_nn(act_ref[:, 2 * lanes : 2 * lanes + ff], up_w[...])
    scalars = act_ref[:, ff:lanes].astype(f32)
    for k, out in enumerate(outs):
        rows = slice(k * cap, (k + 1) * cap)
        out[:, :width] = update[rows].astype(bf16)
        out[:, width : 2 * width] = dnormed[rows].astype(bf16)
        out[:, 2 * width : 2 * width + spare] = scalars[rows].astype(bf16)
        out[:, 2 * width + spare :] = jnp.zeros((cap, out.shape[1] - 2 * width - spare), bf16)


def join_kernel(lanes, parts, *refs):
    acts, taken, (hidden, dgate, dup, pg, cot) = refs[:parts], refs[parts : 2 * parts], refs[2 * parts :]
    ff, width = hidden.shape[1], pg.shape[1]
    start = 0
    for act, rows in zip(acts, taken):
        at = slice(start, start + act.shape[0])
        start += act.shape[0]
        for j, out in enumerate((hidden, dgate, dup)):
            out[at, :] = act[:, j * lanes : j * lanes + ff]
        pg[at, :] = rows[:, :width]
        cot[at, :] = rows[:, width:]


def grad_kernel(tile, count, *refs):
    lefts, rights, outs, buffers, (sem,) = (refs[i * count : (i + 1) * count] for i in range(5))
    copies = []
    for left, right, out, buffer in zip(lefts, rights, outs, buffers):
        for start in range(0, left.shape[1], tile):
            at = slice(start, min(start + tile, left.shape[1]))
            buffer[at, :] = lax.dot_general(
                left[:, at], right[...], (((0,), (0,)), ((), ())), preferred_element_type=f32
            )
            copy = pltpu.make_async_copy(buffer.at[at, :], out.at[at, :], sem.at[len(copies)])
            copy.start()
            copies.append(copy)
    for copy in copies:
        copy.wait()


def last_kernel(want, picked, load, mixed, cot, router, gain, *refs):
    *blocks, updated_ref, grad_ref = refs
    _, width = cot.shape
    sums = blocks[0][...].astype(f32)
    for block in blocks[1:]:
        sums = sums + block[...].astype(f32)
    scalars = sums[:, 2 * width :]
    kind = lax.broadcasted_iota(jnp.int32, scalars.shape, 1) % (2 * PARTS)
    dlogit = jnp.sum(jnp.where(kind < PARTS, scalars, 0.0), axis=1, keepdims=True)
    inner = jnp.sum(jnp.where(kind < PARTS, 0.0, scalars), axis=1, keepdims=True)
    new_rows = (picked[...] + sums[:, :width]).astype(bf16)
    drows = (
        load[:, width : 2 * width].astype(f32)
        + sums[:, width : 2 * width] * gain[...].astype(f32)
        - picked[...] * inner
        + dlogit * router[...].astype(f32)
    ).astype(bf16)
    updated_ref[...] = (mixed[...].astype(f32) + dot_nn(want[...], new_rows)).astype(bf16)
    grad_ref[...] = (cot[...].astype(f32) + dot_nn(want[...], drows)).astype(bf16)


def fast(states, mix_weights, router, norm_gain, gate_weight, up_weight, down_weight, counts, chosen, cotangent):
    slots = lax.axis_size("dp")
    tensor = lax.axis_size("tensor")
    cap = chosen.shape[1]
    tokens, width = cotangent.shape
    ff = gate_weight.shape[1]
    model_width = width * tensor
    lanes = (ff + 2 * PARTS * tensor + 127) // 128 * 128
    columns = 2 * width + 128
    hbm = pl.BlockSpec(memory_space=pltpu.HBM)
    anywhere = pl.BlockSpec(memory_space=pl.ANY)
    block = sds((cap, columns), bf16)

    def over_dp(x, k):
        return lax.ppermute(x, "dp", [(i, i ^ k) for i in range(slots)])

    def over_tensor(x, k):
        return lax.ppermute(x, "tensor", [(i, i ^ k) for i in range(tensor)])

    def copy_of(x, space=pltpu.VMEM):
        return space(x.shape, x.dtype)

    sem = pltpu.SemaphoreType.DMA((8,))
    picked, load = call(
        functools.partial(pick_kernel, cap),
        (sds((cap, width), f32), block),
        [hbm] * 7,
        [copy_of(x, pltpu.SMEM) for x in (counts, chosen, mix_weights)]
        + [copy_of(x) for x in (states, cotangent, router, norm_gain)]
        + [sem],
        vmem=65_000_000,
    )(counts, chosen, mix_weights, states, cotangent, router, norm_gain)
    blocks = {0: load}
    for step in (4, 2, 1):
        for k in list(blocks):
            blocks[k ^ step] = over_dp(blocks[k], step)
    weight = sds((ff, width), bf16)
    weights = call(
        weights_kernel, (weight,) * 3, [anywhere] + [hbm] * 3, [sem], nbytes=13 << 20, vmem=48_000_000,
    )(load, gate_weight.T, up_weight.T, down_weight)

    def summed(chosen_slots):
        part = len(chosen_slots)
        rows, half = part * cap, part * cap // 2
        near = chosen_slots[0] == 0
        own, send, taken = call(
            functools.partial(first_kernel, part, lanes),
            (sds((half, 3 * lanes), f32), sds((half, 3 * lanes), bf16), sds((rows, 2 * width), bf16)),
            [anywhere if near else VMEM] + [VMEM] * (part + 2),
            [pltpu.VMEM((rows, 3 * lanes), f32)] + ([copy_of(load), sem] if near else []),
        )(*[blocks[k] for k in chosen_slots], *weights)
        send, own = call(
            add_kernel, (sds((half, 3 * lanes), bf16), sds((half, 3 * lanes), f32)), [VMEM] * 2
        )(own, over_tensor(send, 1))
        return own, over_tensor(send, 2), taken

    def acted(part, own, got):
        act = call(functools.partial(act_kernel, ff, lanes, model_width), sds(got.shape, bf16), [VMEM] * 2)(own, got)
        *some, act = call(
            functools.partial(second_kernel, part, lanes),
            tuple([block] * part + [sds((part * cap, 3 * lanes), bf16)]),
            [VMEM] * 5,
        )(act, over_tensor(act, 1), *weights)
        return some, act

    mixed, cot_kept, want = call(
        prep_kernel,
        (sds((tokens, width), bf16), sds((tokens, width), bf16), sds((tokens, cap), bf16)),
        [anywhere] + [hbm] * 5,
        [copy_of(x, pltpu.SMEM) for x in (counts, chosen, mix_weights)] + [copy_of(states), copy_of(cotangent), sem],
        nbytes=3 << 20,
    )(load, counts, chosen, mix_weights, states, cotangent)
    chunks = {"near": (0, 1, 2, 3), "mid": (4, 5), "far": (6, 7)}
    sums = {name: summed(some) for name, some in chunks.items()}
    outs, acts, taken = [], [], []
    for name, some in chunks.items():
        own, got, rows_of = sums[name]
        blocks_of, act = acted(len(some), own, got)
        outs += blocks_of
        acts.append(act)
        taken.append(rows_of)

    def moved(value, step):
        return over_dp(value, step).astype(f32)

    def total_of(k, *more):
        return sum(more, outs[k].astype(f32) + moved(outs[k ^ 1], 1)).astype(bf16)

    sum_4 = total_of(4, moved(total_of(6), 2))
    back = [over_dp(outs[1], 1), over_dp(total_of(2), 2), over_dp(sum_4, 4)]
    hidden, dgate, dup, pg, cot = call(
        functools.partial(join_kernel, lanes, len(chunks)),
        tuple([sds((slots * cap, ff), bf16)] * 3 + [sds((slots * cap, width), bf16)] * 2),
        [VMEM] * (2 * len(chunks)),
    )(*acts, *taken)
    tile = 256

    def grads(lefts, rights):
        out = sds((ff, width), f32)
        count = len(lefts)
        return pl.pallas_call(
            functools.partial(grad_kernel, tile, count),
            out_shape=(out,) * count,
            in_specs=[VMEM] * (2 * count),
            out_specs=(anywhere,) * count,
            scratch_shapes=[pltpu.VMEM(out.shape, f32)] * count
            + [pltpu.SemaphoreType.DMA((count * pl.cdiv(ff, tile),))],
            compiler_params=pltpu.CompilerParams(vmem_limit_bytes=32 << 20),
            cost_estimate=pl.CostEstimate(flops=0, bytes_accessed=count * ff * width * 4, transcendentals=0),
        )(*lefts, *rights)

    (grad_down,) = grads((hidden,), (cot,))
    grad_gate, grad_up = (grad.T for grad in grads((dgate, dup), (pg, pg)))
    updated, grad_input = call(
        last_kernel, (sds((tokens, width), bf16), sds((tokens, width), bf16)), [VMEM] * 11
    )(want, picked, load, mixed, cot_kept, router.reshape(1, width), norm_gain.reshape(1, width), outs[0], *back)
    return updated, grad_input, grad_gate, grad_up, grad_down


def general(
    states,
    mix_weights,
    router,
    norm_gain,
    gate_weight,
    up_weight,
    down_weight,
    counts,
    chosen,
    cotangent,
):
    width_here = cotangent.shape[1]
    my_rank = lax.axis_index("dp")
    model_width = width_here * lax.axis_size("tensor")
    mixed = jnp.tensordot(mix_weights, states.astype(jnp.float32), axes=1)
    flat_counts = counts.reshape(-1)
    my_count = flat_counts[my_rank]
    positions = chosen[0]
    capacity = positions.shape[0]
    slot_ids = jnp.arange(capacity, dtype=jnp.int32)
    is_valid = slot_ids < my_count
    valid = is_valid.astype(jnp.float32)[:, None]
    picked = mixed[positions]
    router_float = router.astype(jnp.float32)
    gain_float = norm_gain.astype(jnp.float32)
    logit_part = jnp.sum(picked * router_float, axis=1)
    square_part = jnp.sum(picked * picked, axis=1)
    logits, squares = lax.psum((logit_part, square_part), "tensor")
    gating = jax.nn.sigmoid(logits)
    inverse = lax.rsqrt(squares / model_width + epsilon)
    normed = (picked * inverse[:, None] * gain_float * valid).astype(jnp.bfloat16)
    gathered = lax.all_gather(normed, "dp", axis=0, tiled=True)
    gate_part = jnp.dot(gathered, gate_weight, preferred_element_type=jnp.float32)
    up_part = jnp.dot(gathered, up_weight, preferred_element_type=jnp.float32)
    gate_pre, up_pre = lax.psum((gate_part, up_part), "tensor")
    hidden = (jax.nn.silu(gate_pre) * up_pre).astype(jnp.bfloat16)
    update_work = lax.psum_scatter(
        jnp.dot(hidden, down_weight, preferred_element_type=jnp.float32),
        "dp",
        scatter_dimension=0,
        tiled=True,
    ).astype(jnp.bfloat16)
    update_float = update_work.astype(jnp.float32) * valid
    new_rows = picked + gating[:, None] * update_float
    result = mixed.at[positions].set(new_rows).astype(jnp.bfloat16)
    cot_rows = cotangent[positions].astype(jnp.float32)
    dupdate = (gating[:, None] * cot_rows * valid).astype(jnp.bfloat16)
    dlogit_part = jnp.sum(cot_rows * update_float, axis=1)
    dgathered = lax.all_gather(dupdate, "dp", axis=0, tiled=True)
    dhidden_part = jnp.dot(dgathered, down_weight.T, preferred_element_type=jnp.float32)
    dhidden = lax.psum(dhidden_part, "tensor")
    sigmoid_pre = jax.nn.sigmoid(gate_pre)
    dgate_pre = (dhidden * up_pre * sigmoid_pre * (1.0 + gate_pre * (1.0 - sigmoid_pre))).astype(
        jnp.bfloat16
    )
    dup_pre = (dhidden * gate_pre * sigmoid_pre).astype(jnp.bfloat16)
    grad_down = jnp.dot(hidden.T, dgathered, preferred_element_type=jnp.float32)
    grad_gate = jnp.dot(gathered.T, dgate_pre, preferred_element_type=jnp.float32)
    grad_up = jnp.dot(gathered.T, dup_pre, preferred_element_type=jnp.float32)
    first_term = jnp.dot(dgate_pre, gate_weight.T, preferred_element_type=jnp.float32)
    dnormed_work = lax.psum_scatter(
        first_term + jnp.dot(dup_pre, up_weight.T, preferred_element_type=jnp.float32),
        "dp",
        scatter_dimension=0,
        tiled=True,
    )
    scaled = dnormed_work * gain_float * valid
    inner_part = jnp.sum(scaled * picked, axis=1)
    dlogit_sum, inner_sum = lax.psum((dlogit_part, inner_part), "tensor")
    dlogit = dlogit_sum * gating * (1.0 - gating)
    drows = (
        cot_rows
        + inverse[:, None] * scaled
        - picked * (inverse**3 * inner_sum / model_width)[:, None]
        + valid * dlogit[:, None] * router_float
    )
    grad_input = cotangent.astype(jnp.float32).at[positions].set(drows).astype(jnp.bfloat16)
    return (result, grad_input, grad_gate, grad_up, grad_down)


def solution(mesh):
    small = (mesh.shape["dp"], mesh.shape["tensor"]) == (8, 4)
    return jax.shard_map(
        fast if small else general,
        mesh=mesh,
        in_specs=(
            P(None, "dp", "tensor"),
            P(),
            P("tensor"),
            P("tensor"),
            P("tensor", "dp"),
            P("tensor", "dp"),
            P("dp", "tensor"),
            P(),
            P("dp", None),
            P("dp", "tensor"),
        ),
        out_specs=(
            P("dp", "tensor"),
            P("dp", "tensor"),
            P("tensor", "dp"),
            P("tensor", "dp"),
            P("dp", "tensor"),
        ),
        check_vma=False,
    )
```

```python
import functools
import jax
import jax.numpy as jnp
from jax import lax
from jax.experimental import pallas as pl
from jax.experimental.pallas import tpu as pltpu
from jax.sharding import PartitionSpec as P


epsilon = 1e-05
f32, bf16 = jnp.float32, jnp.bfloat16
SMEM = pl.BlockSpec(memory_space=pltpu.SMEM)
VMEM = pl.BlockSpec(memory_space=pltpu.VMEM)
PARTS = 3


def call(kernel, out, ins, scratch=(), flops=0, nbytes=0, vmem=32 << 20):
    return pl.pallas_call(
        kernel,
        out_shape=out,
        in_specs=ins,
        out_specs=jax.tree.map(lambda _: VMEM, out),
        scratch_shapes=list(scratch),
        cost_estimate=pl.CostEstimate(flops=flops, bytes_accessed=nbytes, transcendentals=0),
        compiler_params=pltpu.CompilerParams(vmem_limit_bytes=vmem),
    )


def sds(shape, dtype):
    return jax.ShapeDtypeStruct(shape, dtype)


def terms(value):
    out, rest = [], value
    for _ in range(PARTS):
        term = rest.astype(bf16).astype(f32)
        out.append(term)
        rest = rest - term
    return out


def in_lanes(values, width, first):
    rows = values[0].shape[0]
    lane = lax.broadcasted_iota(jnp.int32, (rows, width), 1)
    total = jnp.zeros((rows, width), f32)
    for i, value in enumerate(values):
        total = jnp.where(lane == first + i, value, total)
    return total


def dot_nt(a, b):
    return lax.dot_general(a, b, (((1,), (1,)), ((), ())), preferred_element_type=f32)


def dot_nn(a, b):
    return jnp.dot(a, b, preferred_element_type=f32)


def fetch(pairs, sem):
    copies = [pltpu.make_async_copy(src, dst, sem.at[i]) for i, (src, dst) in enumerate(pairs)]
    for copy in copies:
        copy.start()
    return copies


def pick_kernel(cap, counts, chosen, mixw, states, cot, router, gain, picked_ref, load_ref, *scratch):
    *places, sem = scratch
    for copy in fetch(list(zip((counts, chosen, mixw, states, cot, router, gain), places)), sem):
        copy.wait()
    counts, chosen, mixw, states, cot, router, gain = places
    mine = counts[0, lax.axis_index("dp")]
    tokens, width = cot.shape
    row = lax.broadcasted_iota(jnp.int32, (cap, tokens), 0)
    col = lax.broadcasted_iota(jnp.int32, (cap, tokens), 1)
    want = jnp.zeros((cap, tokens), f32)
    for k in range(cap):
        want = jnp.where((row == k) & (col == chosen[0, k]) & (k < mine), 1.0, want)
    want = want.astype(bf16)
    picked = mixw[0] * dot_nn(want, states[0])
    for j in range(1, states.shape[0]):
        picked = picked + mixw[j] * dot_nn(want, states[j])
    picked_ref[...] = picked
    load_ref[:, :width] = (picked * gain[...].astype(f32).reshape(1, width)).astype(bf16)
    load_ref[:, width : 2 * width] = dot_nn(want, cot[...]).astype(bf16)
    logit = jnp.sum(picked * router[...].astype(f32).reshape(1, width), axis=1, keepdims=True)
    square = jnp.sum(picked * picked, axis=1, keepdims=True)
    first = 2 * PARTS * lax.axis_index("tensor")
    load_ref[:, 2 * width :] = in_lanes(terms(logit) + terms(square), 128, first).astype(bf16)


def weights_kernel(*refs):
    *pairs, sem = refs
    half = len(pairs) // 2
    for copy in fetch(list(zip(pairs[:half], pairs[half:])), sem):
        copy.wait()


def prep_kernel(counts, chosen, mixw, states, cot, *refs):
    mixed_ref, cot_ref, want_ref, *places, sem = refs
    for copy in fetch(list(zip((counts, chosen, mixw, states, cot), places)), sem):
        copy.wait()
    counts, chosen, mixw, states, cot = places
    mine = counts[0, lax.axis_index("dp")]
    tokens, cap = want_ref.shape
    row = lax.broadcasted_iota(jnp.int32, (tokens, cap), 0)
    col = lax.broadcasted_iota(jnp.int32, (tokens, cap), 1)
    want = jnp.zeros((tokens, cap), f32)
    for k in range(cap):
        want = jnp.where((col == k) & (row == chosen[0, k]) & (k < mine), 1.0, want)
    want_ref[...] = want.astype(bf16)
    keep = jnp.sum(want, axis=1, keepdims=True) == 0.0
    mixed = mixw[0] * states[0].astype(f32)
    for j in range(1, states.shape[0]):
        mixed = mixed + mixw[j] * states[j].astype(f32)
    mixed_ref[...] = jnp.where(keep, mixed, 0.0).astype(bf16)
    cot_ref[...] = jnp.where(keep, cot[...].astype(f32), 0.0).astype(bf16)


def first_kernel(slots, lanes, *refs):
    blocks, (gate_w, up_w, down_w, own_ref, send_ref, rows_ref, sums_ref) = refs[:slots], refs[slots : slots + 7]
    if len(refs) > slots + 7:
        mine_ref, sem = refs[slots + 7 :]
        (copy,) = fetch([(blocks[0], mine_ref)], sem)
        copy.wait()
        blocks = (mine_ref,) + blocks[1:]
    core = lax.axis_index("tensor") % 2
    ff, width = gate_w.shape
    rows = jnp.concatenate([block[...].astype(f32) for block in blocks], axis=0)
    spare = lanes - ff
    zeros = jnp.zeros((rows.shape[0], spare), f32)
    sums_ref[:, ff:lanes] = rows[:, 2 * width : 2 * width + spare]
    rows_ref[...] = rows[:, : 2 * width].astype(bf16)
    pg = rows_ref[:, :width]
    sums_ref[:, :ff] = dot_nt(pg, gate_w[...])
    sums_ref[:, lanes : lanes + ff] = dot_nt(pg, up_w[...])
    sums_ref[:, lanes + ff : 2 * lanes] = zeros
    sums_ref[:, 2 * lanes : 2 * lanes + ff] = dot_nt(rows_ref[:, width:], down_w[...])
    sums_ref[:, 2 * lanes + ff :] = zeros
    half = own_ref.shape[0]
    own_ref[...] = sums_ref[pl.ds(pl.multiple_of(core * half, 8), half), :]
    send_ref[...] = sums_ref[pl.ds(pl.multiple_of((1 - core) * half, 8), half), :].astype(bf16)


def add_kernel(own, got, out_ref, sum_ref):
    total = own[...] + got[...].astype(f32)
    sum_ref[...] = total
    out_ref[...] = total.astype(bf16)


def act_kernel(ff, lanes, model_width, own, got, out_ref):
    def part(i, size=ff, at=0):
        return own[:, i * lanes + at : i * lanes + at + size] + got[
            :, i * lanes + at : i * lanes + at + size
        ].astype(f32)

    scalars = part(0, lanes - ff, ff)
    kind = lax.broadcasted_iota(jnp.int32, scalars.shape, 1) % (2 * PARTS)
    logits = jnp.sum(jnp.where(kind < PARTS, scalars, 0.0), axis=1, keepdims=True)
    squares = jnp.sum(jnp.where(kind < PARTS, 0.0, scalars), axis=1, keepdims=True)
    gating = jax.nn.sigmoid(logits)
    inverse = lax.rsqrt(squares / model_width + epsilon)
    gate_raw, up_raw, dh_raw = part(0), part(1), part(2)
    gate_pre, up_pre = gate_raw * inverse, up_raw * inverse
    dhidden = dh_raw * gating
    sig = jax.nn.sigmoid(gate_pre)
    silu = gate_pre * sig
    hidden = (gating * silu * up_pre).astype(bf16)
    scaled = dhidden * inverse
    dgate = (scaled * up_pre * sig * (1.0 + gate_pre * (1.0 - sig))).astype(bf16)
    dup = (scaled * silu).astype(bf16)
    dlogit = (1.0 - gating) * jnp.sum(hidden.astype(f32) * dh_raw, axis=1, keepdims=True)
    inner = jnp.sum(dgate.astype(f32) * gate_raw + dup.astype(f32) * up_raw, axis=1, keepdims=True)
    inner = inner * inverse * inverse / model_width
    spare = lanes - ff
    zeros = jnp.zeros((own.shape[0], spare), bf16)
    first = 2 * PARTS * (lax.axis_index("dp") % 4)
    out_ref[:, :ff] = hidden
    out_ref[:, ff:lanes] = in_lanes(terms(dlogit) + terms(inner), spare, first).astype(bf16)
    out_ref[:, lanes : lanes + ff] = dgate
    out_ref[:, lanes + ff : 2 * lanes] = zeros
    out_ref[:, 2 * lanes : 2 * lanes + ff] = dup
    out_ref[:, 2 * lanes + ff :] = zeros


def second_kernel(slots, lanes, own, got, gate_w, up_w, down_w, *refs):
    outs, (act_ref,) = refs[:slots], refs[slots:]
    core = lax.axis_index("tensor") % 2
    ff, width = gate_w.shape
    cap = outs[0].shape[0]
    mine, other = own[...].astype(f32), got[...].astype(f32)
    order = (jnp.where(core == 0, mine, other), jnp.where(core == 0, other, mine))
    act_ref[...] = jnp.concatenate(order, axis=0).astype(bf16)
    spare = lanes - ff
    update = dot_nn(act_ref[:, :ff], down_w[...])
    dnormed = dot_nn(act_ref[:, lanes : lanes + ff], gate_w[...])
    dnormed = dnormed + dot_nn(act_ref[:, 2 * lanes : 2 * lanes + ff], up_w[...])
    scalars = act_ref[:, ff:lanes].astype(f32)
    for k, out in enumerate(outs):
        rows = slice(k * cap, (k + 1) * cap)
        out[:, :width] = update[rows].astype(bf16)
        out[:, width : 2 * width] = dnormed[rows].astype(bf16)
        out[:, 2 * width : 2 * width + spare] = scalars[rows].astype(bf16)
        out[:, 2 * width + spare :] = jnp.zeros((cap, out.shape[1] - 2 * width - spare), bf16)


def join_kernel(lanes, parts, *refs):
    acts, taken, (hidden, dgate, dup, pg, cot) = refs[:parts], refs[parts : 2 * parts], refs[2 * parts :]
    ff, width = hidden.shape[1], pg.shape[1]
    start = 0
    for act, rows in zip(acts, taken):
        at = slice(start, start + act.shape[0])
        start += act.shape[0]
        for j, out in enumerate((hidden, dgate, dup)):
            out[at, :] = act[:, j * lanes : j * lanes + ff]
        pg[at, :] = rows[:, :width]
        cot[at, :] = rows[:, width:]


def grad_kernel(tile, count, *refs):
    lefts, rights, outs, buffers, (sem,) = (refs[i * count : (i + 1) * count] for i in range(5))
    copies = []
    for left, right, out, buffer in zip(lefts, rights, outs, buffers):
        for start in range(0, left.shape[1], tile):
            at = slice(start, min(start + tile, left.shape[1]))
            buffer[at, :] = lax.dot_general(
                left[:, at], right[...], (((0,), (0,)), ((), ())), preferred_element_type=f32
            )
            copy = pltpu.make_async_copy(buffer.at[at, :], out.at[at, :], sem.at[len(copies)])
            copy.start()
            copies.append(copy)
    for copy in copies:
        copy.wait()


def last_kernel(want, picked, taken, mixed, cot, router, gain, *refs):
    *blocks, updated_ref, grad_ref = refs
    _, width = cot.shape
    sums = blocks[0][...].astype(f32)
    for block in blocks[1:]:
        sums = sums + block[...].astype(f32)
    scalars = sums[:, 2 * width :]
    kind = lax.broadcasted_iota(jnp.int32, scalars.shape, 1) % (2 * PARTS)
    dlogit = jnp.sum(jnp.where(kind < PARTS, scalars, 0.0), axis=1, keepdims=True)
    inner = jnp.sum(jnp.where(kind < PARTS, 0.0, scalars), axis=1, keepdims=True)
    new_rows = (picked[...] + sums[:, :width]).astype(bf16)
    drows = (
        taken[: picked.shape[0], width:].astype(f32)
        + sums[:, width : 2 * width] * gain[...].astype(f32)
        - picked[...] * inner
        + dlogit * router[...].astype(f32)
    ).astype(bf16)
    updated_ref[...] = (mixed[...].astype(f32) + dot_nn(want[...], new_rows)).astype(bf16)
    grad_ref[...] = (cot[...].astype(f32) + dot_nn(want[...], drows)).astype(bf16)


def fast(states, mix_weights, router, norm_gain, gate_weight, up_weight, down_weight, counts, chosen, cotangent):
    slots = lax.axis_size("dp")
    tensor = lax.axis_size("tensor")
    cap = chosen.shape[1]
    tokens, width = cotangent.shape
    ff = gate_weight.shape[1]
    model_width = width * tensor
    lanes = (ff + 2 * PARTS * tensor + 127) // 128 * 128
    columns = 2 * width + 128
    hbm = pl.BlockSpec(memory_space=pltpu.HBM)
    anywhere = pl.BlockSpec(memory_space=pl.ANY)
    block = sds((cap, columns), bf16)

    def over_dp(x, k):
        return lax.ppermute(x, "dp", [(i, i ^ k) for i in range(slots)])

    def over_tensor(x, k):
        return lax.ppermute(x, "tensor", [(i, i ^ k) for i in range(tensor)])

    def copy_of(x, space=pltpu.VMEM):
        return space(x.shape, x.dtype)

    sem = pltpu.SemaphoreType.DMA((8,))
    picked, load = call(
        functools.partial(pick_kernel, cap),
        (sds((cap, width), f32), block),
        [hbm] * 7,
        [copy_of(x, pltpu.SMEM) for x in (counts, chosen, mix_weights)]
        + [copy_of(x) for x in (states, cotangent, router, norm_gain)]
        + [sem],
        vmem=65_000_000,
    )(counts, chosen, mix_weights, states, cotangent, router, norm_gain)
    blocks = {0: load}
    for step in (4, 2, 1):
        for k in list(blocks):
            blocks[k ^ step] = over_dp(blocks[k], step)
    weight = sds((ff, width), bf16)
    weights = call(
        weights_kernel, (weight,) * 3, [hbm] * 3, [sem], nbytes=13 << 20, vmem=48_000_000,
    )(gate_weight.T, up_weight.T, down_weight)
    mixed, cot_kept, want = call(
        prep_kernel,
        (sds((tokens, width), bf16), sds((tokens, width), bf16), sds((tokens, cap), bf16)),
        [hbm] * 5,
        [copy_of(x, pltpu.SMEM) for x in (counts, chosen, mix_weights)] + [copy_of(states), copy_of(cotangent), sem],
        nbytes=3 << 20,
    )(counts, chosen, mix_weights, states, cotangent)

    def summed(chosen_slots):
        part = len(chosen_slots)
        rows, half = part * cap, part * cap // 2
        near = chosen_slots[0] == 0
        own, send, taken = call(
            functools.partial(first_kernel, part, lanes),
            (sds((half, 3 * lanes), f32), sds((half, 3 * lanes), bf16), sds((rows, 2 * width), bf16)),
            [anywhere if near else VMEM] + [VMEM] * (part + 2),
            [pltpu.VMEM((rows, 3 * lanes), f32)] + ([copy_of(load), sem] if near else []),
        )(*[blocks[k] for k in chosen_slots], *weights)
        send, own = call(
            add_kernel, (sds((half, 3 * lanes), bf16), sds((half, 3 * lanes), f32)), [VMEM] * 2
        )(own, over_tensor(send, 1))
        return own, over_tensor(send, 2), taken

    def acted(part, own, got):
        act = call(
            functools.partial(act_kernel, ff, lanes, model_width), sds(got.shape, bf16), [VMEM] * 2
        )(own, got)
        *some, act = call(
            functools.partial(second_kernel, part, lanes),
            tuple([block] * part + [sds((part * cap, 3 * lanes), bf16)]),
            [VMEM] * 5,
        )(act, over_tensor(act, 1), *weights)
        return some, act

    chunks = {"n": (0, 1, 2, 3), "m": (4, 5), "f": (6, 7)}
    sums = {name: summed(some) for name, some in chunks.items()}
    outs, acts, taken = [], [], []
    for name, some in chunks.items():
        own, got, rows_of = sums[name]
        blocks_of, act = acted(len(some), own, got)
        outs += blocks_of
        acts.append(act)
        taken.append(rows_of)

    def moved(value, step):
        return over_dp(value, step).astype(f32)

    def total_of(k, *more):
        return sum(more, outs[k].astype(f32) + moved(outs[k ^ 1], 1)).astype(bf16)

    sum_4 = total_of(4, moved(total_of(6), 2))
    back = [over_dp(outs[1], 1), over_dp(total_of(2), 2), over_dp(sum_4, 4)]
    hidden, dgate, dup, pg, cot = call(
        functools.partial(join_kernel, lanes, len(chunks)),
        tuple([sds((slots * cap, ff), bf16)] * 3 + [sds((slots * cap, width), bf16)] * 2),
        [VMEM] * (2 * len(chunks)),
    )(*acts, *taken)
    tile = 256

    def grads(lefts, rights):
        out = sds((ff, width), f32)
        count = len(lefts)
        return pl.pallas_call(
            functools.partial(grad_kernel, tile, count),
            out_shape=(out,) * count,
            in_specs=[VMEM] * (2 * count),
            out_specs=(anywhere,) * count,
            scratch_shapes=[pltpu.VMEM(out.shape, f32)] * count
            + [pltpu.SemaphoreType.DMA((count * pl.cdiv(ff, tile),))],
            compiler_params=pltpu.CompilerParams(vmem_limit_bytes=32 << 20),
            cost_estimate=pl.CostEstimate(flops=0, bytes_accessed=count * ff * width * 4, transcendentals=0),
        )(*lefts, *rights)

    (grad_down,) = grads((hidden,), (cot,))
    grad_gate, grad_up = (grad.T for grad in grads((dgate, dup), (pg, pg)))
    updated, grad_input = call(
        last_kernel, (sds((tokens, width), bf16), sds((tokens, width), bf16)), [VMEM] * 11
    )(want, picked, taken[0], mixed, cot_kept, router.reshape(1, width), norm_gain.reshape(1, width), outs[0], *back)
    return updated, grad_input, grad_gate, grad_up, grad_down


def general(
    states,
    mix_weights,
    router,
    norm_gain,
    gate_weight,
    up_weight,
    down_weight,
    counts,
    chosen,
    cotangent,
):
    width_here = cotangent.shape[1]
    my_rank = lax.axis_index("dp")
    model_width = width_here * lax.axis_size("tensor")
    mixed = jnp.tensordot(mix_weights, states.astype(jnp.float32), axes=1)
    flat_counts = counts.reshape(-1)
    my_count = flat_counts[my_rank]
    positions = chosen[0]
    capacity = positions.shape[0]
    slot_ids = jnp.arange(capacity, dtype=jnp.int32)
    is_valid = slot_ids < my_count
    valid = is_valid.astype(jnp.float32)[:, None]
    picked = mixed[positions]
    router_float = router.astype(jnp.float32)
    gain_float = norm_gain.astype(jnp.float32)
    logit_part = jnp.sum(picked * router_float, axis=1)
    square_part = jnp.sum(picked * picked, axis=1)
    logits, squares = lax.psum((logit_part, square_part), "tensor")
    gating = jax.nn.sigmoid(logits)
    inverse = lax.rsqrt(squares / model_width + epsilon)
    normed = (picked * inverse[:, None] * gain_float * valid).astype(jnp.bfloat16)
    gathered = lax.all_gather(normed, "dp", axis=0, tiled=True)
    gate_part = jnp.dot(gathered, gate_weight, preferred_element_type=jnp.float32)
    up_part = jnp.dot(gathered, up_weight, preferred_element_type=jnp.float32)
    gate_pre, up_pre = lax.psum((gate_part, up_part), "tensor")
    hidden = (jax.nn.silu(gate_pre) * up_pre).astype(jnp.bfloat16)
    update_work = lax.psum_scatter(
        jnp.dot(hidden, down_weight, preferred_element_type=jnp.float32),
        "dp",
        scatter_dimension=0,
        tiled=True,
    ).astype(jnp.bfloat16)
    update_float = update_work.astype(jnp.float32) * valid
    new_rows = picked + gating[:, None] * update_float
    result = mixed.at[positions].set(new_rows).astype(jnp.bfloat16)
    cot_rows = cotangent[positions].astype(jnp.float32)
    dupdate = (gating[:, None] * cot_rows * valid).astype(jnp.bfloat16)
    dlogit_part = jnp.sum(cot_rows * update_float, axis=1)
    dgathered = lax.all_gather(dupdate, "dp", axis=0, tiled=True)
    dhidden_part = jnp.dot(dgathered, down_weight.T, preferred_element_type=jnp.float32)
    dhidden = lax.psum(dhidden_part, "tensor")
    sigmoid_pre = jax.nn.sigmoid(gate_pre)
    dgate_pre = (dhidden * up_pre * sigmoid_pre * (1.0 + gate_pre * (1.0 - sigmoid_pre))).astype(
        jnp.bfloat16
    )
    dup_pre = (dhidden * gate_pre * sigmoid_pre).astype(jnp.bfloat16)
    grad_down = jnp.dot(hidden.T, dgathered, preferred_element_type=jnp.float32)
    grad_gate = jnp.dot(gathered.T, dgate_pre, preferred_element_type=jnp.float32)
    grad_up = jnp.dot(gathered.T, dup_pre, preferred_element_type=jnp.float32)
    first_term = jnp.dot(dgate_pre, gate_weight.T, preferred_element_type=jnp.float32)
    dnormed_work = lax.psum_scatter(
        first_term + jnp.dot(dup_pre, up_weight.T, preferred_element_type=jnp.float32),
        "dp",
        scatter_dimension=0,
        tiled=True,
    )
    scaled = dnormed_work * gain_float * valid
    inner_part = jnp.sum(scaled * picked, axis=1)
    dlogit_sum, inner_sum = lax.psum((dlogit_part, inner_part), "tensor")
    dlogit = dlogit_sum * gating * (1.0 - gating)
    drows = (
        cot_rows
        + inverse[:, None] * scaled
        - picked * (inverse**3 * inner_sum / model_width)[:, None]
        + valid * dlogit[:, None] * router_float
    )
    grad_input = cotangent.astype(jnp.float32).at[positions].set(drows).astype(jnp.bfloat16)
    return (result, grad_input, grad_gate, grad_up, grad_down)


def solution(mesh):
    small = (mesh.shape["dp"], mesh.shape["tensor"]) == (8, 4)
    return jax.shard_map(
        fast if small else general,
        mesh=mesh,
        in_specs=(
            P(None, "dp", "tensor"),
            P(),
            P("tensor"),
            P("tensor"),
            P("tensor", "dp"),
            P("tensor", "dp"),
            P("dp", "tensor"),
            P(),
            P("dp", None),
            P("dp", "tensor"),
        ),
        out_specs=(
            P("dp", "tensor"),
            P("dp", "tensor"),
            P("tensor", "dp"),
            P("tensor", "dp"),
            P("dp", "tensor"),
        ),
        check_vma=False,
    )
```

```python
import functools
import jax
import jax.numpy as jnp
from jax import lax
from jax.experimental import pallas as pl
from jax.experimental.pallas import tpu as pltpu
from jax.sharding import PartitionSpec as P


epsilon = 1e-05
f32, bf16 = jnp.float32, jnp.bfloat16
SMEM = pl.BlockSpec(memory_space=pltpu.SMEM)
VMEM = pl.BlockSpec(memory_space=pltpu.VMEM)
PARTS = 3


def call(kernel, out, ins, scratch=(), flops=0, nbytes=0, vmem=32 << 20):
    return pl.pallas_call(
        kernel,
        out_shape=out,
        in_specs=ins,
        out_specs=jax.tree.map(lambda _: VMEM, out),
        scratch_shapes=list(scratch),
        cost_estimate=pl.CostEstimate(flops=flops, bytes_accessed=nbytes, transcendentals=0),
        compiler_params=pltpu.CompilerParams(vmem_limit_bytes=vmem),
    )


def sds(shape, dtype):
    return jax.ShapeDtypeStruct(shape, dtype)


def terms(value):
    out, rest = [], value
    for _ in range(PARTS):
        term = rest.astype(bf16).astype(f32)
        out.append(term)
        rest = rest - term
    return out


def in_lanes(values, width, first):
    rows = values[0].shape[0]
    lane = lax.broadcasted_iota(jnp.int32, (rows, width), 1)
    total = jnp.zeros((rows, width), f32)
    for i, value in enumerate(values):
        total = jnp.where(lane == first + i, value, total)
    return total


def dot_nt(a, b):
    return lax.dot_general(a, b, (((1,), (1,)), ((), ())), preferred_element_type=f32)


def dot_nn(a, b):
    return jnp.dot(a, b, preferred_element_type=f32)


def fetch(pairs, sem):
    copies = [pltpu.make_async_copy(src, dst, sem.at[i]) for i, (src, dst) in enumerate(pairs)]
    for copy in copies:
        copy.start()
    return copies


def pick_kernel(cap, counts, chosen, mixw, states, cot, router, gain, picked_ref, load_ref, *scratch):
    *places, sem = scratch
    for copy in fetch(list(zip((counts, chosen, mixw, states, cot, router, gain), places)), sem):
        copy.wait()
    counts, chosen, mixw, states, cot, router, gain = places
    mine = counts[0, lax.axis_index("dp")]
    tokens, width = cot.shape
    row = lax.broadcasted_iota(jnp.int32, (cap, tokens), 0)
    col = lax.broadcasted_iota(jnp.int32, (cap, tokens), 1)
    want = jnp.zeros((cap, tokens), f32)
    for k in range(cap):
        want = jnp.where((row == k) & (col == chosen[0, k]) & (k < mine), 1.0, want)
    want = want.astype(bf16)
    picked = mixw[0] * dot_nn(want, states[0])
    for j in range(1, states.shape[0]):
        picked = picked + mixw[j] * dot_nn(want, states[j])
    picked_ref[...] = picked
    load_ref[:, :width] = (picked * gain[...].astype(f32).reshape(1, width)).astype(bf16)
    load_ref[:, width : 2 * width] = dot_nn(want, cot[...]).astype(bf16)
    logit = jnp.sum(picked * router[...].astype(f32).reshape(1, width), axis=1, keepdims=True)
    square = jnp.sum(picked * picked, axis=1, keepdims=True)
    first = 2 * PARTS * lax.axis_index("tensor")
    load_ref[:, 2 * width :] = in_lanes(terms(logit) + terms(square), 128, first).astype(bf16)


def weights_kernel(*refs):
    *pairs, sem = refs
    half = len(pairs) // 2
    for copy in fetch(list(zip(pairs[:half], pairs[half:])), sem):
        copy.wait()


def prep_kernel(counts, chosen, mixw, states, cot, *refs):
    mixed_ref, cot_ref, want_ref, *places, sem = refs
    for copy in fetch(list(zip((counts, chosen, mixw, states, cot), places)), sem):
        copy.wait()
    counts, chosen, mixw, states, cot = places
    mine = counts[0, lax.axis_index("dp")]
    tokens, cap = want_ref.shape
    row = lax.broadcasted_iota(jnp.int32, (tokens, cap), 0)
    col = lax.broadcasted_iota(jnp.int32, (tokens, cap), 1)
    want = jnp.zeros((tokens, cap), f32)
    for k in range(cap):
        want = jnp.where((col == k) & (row == chosen[0, k]) & (k < mine), 1.0, want)
    want_ref[...] = want.astype(bf16)
    keep = jnp.sum(want, axis=1, keepdims=True) == 0.0
    mixed = mixw[0] * states[0].astype(f32)
    for j in range(1, states.shape[0]):
        mixed = mixed + mixw[j] * states[j].astype(f32)
    mixed_ref[...] = jnp.where(keep, mixed, 0.0).astype(bf16)
    cot_ref[...] = jnp.where(keep, cot[...].astype(f32), 0.0).astype(bf16)


def first_kernel(slots, lanes, *refs):
    blocks, (gate_w, up_w, down_w, own_ref, send_ref, rows_ref, sums_ref) = refs[:slots], refs[slots:]
    core = lax.axis_index("tensor") % 2
    ff, width = gate_w.shape
    rows = jnp.concatenate([block[...].astype(f32) for block in blocks], axis=0)
    spare = lanes - ff
    zeros = jnp.zeros((rows.shape[0], spare), f32)
    sums_ref[:, ff:lanes] = rows[:, 2 * width : 2 * width + spare]
    rows_ref[...] = rows[:, : 2 * width].astype(bf16)
    pg = rows_ref[:, :width]
    sums_ref[:, :ff] = dot_nt(pg, gate_w[...])
    sums_ref[:, lanes : lanes + ff] = dot_nt(pg, up_w[...])
    sums_ref[:, lanes + ff : 2 * lanes] = zeros
    sums_ref[:, 2 * lanes : 2 * lanes + ff] = dot_nt(rows_ref[:, width:], down_w[...])
    sums_ref[:, 2 * lanes + ff :] = zeros
    half = own_ref.shape[0]
    own_ref[...] = sums_ref[pl.ds(pl.multiple_of(core * half, 8), half), :]
    send_ref[...] = sums_ref[pl.ds(pl.multiple_of((1 - core) * half, 8), half), :].astype(bf16)


def add_kernel(own, got, out_ref, sum_ref):
    total = own[...] + got[...].astype(f32)
    sum_ref[...] = total
    out_ref[...] = total.astype(bf16)


def act_kernel(ff, lanes, model_width, own, got, out_ref):
    def part(i, size=ff, at=0):
        return own[:, i * lanes + at : i * lanes + at + size] + got[
            :, i * lanes + at : i * lanes + at + size
        ].astype(f32)

    scalars = part(0, lanes - ff, ff)
    kind = lax.broadcasted_iota(jnp.int32, scalars.shape, 1) % (2 * PARTS)
    logits = jnp.sum(jnp.where(kind < PARTS, scalars, 0.0), axis=1, keepdims=True)
    squares = jnp.sum(jnp.where(kind < PARTS, 0.0, scalars), axis=1, keepdims=True)
    gating = jax.nn.sigmoid(logits)
    inverse = lax.rsqrt(squares / model_width + epsilon)
    gate_raw, up_raw, dh_raw = part(0), part(1), part(2)
    gate_pre, up_pre = gate_raw * inverse, up_raw * inverse
    dhidden = dh_raw * gating
    sig = jax.nn.sigmoid(gate_pre)
    silu = gate_pre * sig
    hidden = (gating * silu * up_pre).astype(bf16)
    scaled = dhidden * inverse
    dgate = (scaled * up_pre * sig * (1.0 + gate_pre * (1.0 - sig))).astype(bf16)
    dup = (scaled * silu).astype(bf16)
    dlogit = (1.0 - gating) * jnp.sum(hidden.astype(f32) * dh_raw, axis=1, keepdims=True)
    inner = jnp.sum(dgate.astype(f32) * gate_raw + dup.astype(f32) * up_raw, axis=1, keepdims=True)
    inner = inner * inverse * inverse / model_width
    spare = lanes - ff
    zeros = jnp.zeros((own.shape[0], spare), bf16)
    first = 2 * PARTS * (lax.axis_index("dp") % 4)
    out_ref[:, :ff] = hidden
    out_ref[:, ff:lanes] = in_lanes(terms(dlogit) + terms(inner), spare, first).astype(bf16)
    out_ref[:, lanes : lanes + ff] = dgate
    out_ref[:, lanes + ff : 2 * lanes] = zeros
    out_ref[:, 2 * lanes : 2 * lanes + ff] = dup
    out_ref[:, 2 * lanes + ff :] = zeros


def second_kernel(slots, lanes, own, got, gate_w, up_w, down_w, *refs):
    outs, (act_ref,) = refs[:slots], refs[slots:]
    core = lax.axis_index("tensor") % 2
    ff, width = gate_w.shape
    cap = outs[0].shape[0]
    mine, other = own[...].astype(f32), got[...].astype(f32)
    order = (jnp.where(core == 0, mine, other), jnp.where(core == 0, other, mine))
    act_ref[...] = jnp.concatenate(order, axis=0).astype(bf16)
    spare = lanes - ff
    update = dot_nn(act_ref[:, :ff], down_w[...])
    dnormed = dot_nn(act_ref[:, lanes : lanes + ff], gate_w[...])
    dnormed = dnormed + dot_nn(act_ref[:, 2 * lanes : 2 * lanes + ff], up_w[...])
    scalars = act_ref[:, ff:lanes].astype(f32)
    for k, out in enumerate(outs):
        rows = slice(k * cap, (k + 1) * cap)
        out[:, :width] = update[rows].astype(bf16)
        out[:, width : 2 * width] = dnormed[rows].astype(bf16)
        out[:, 2 * width : 2 * width + spare] = scalars[rows].astype(bf16)
        out[:, 2 * width + spare :] = jnp.zeros((cap, out.shape[1] - 2 * width - spare), bf16)


def join_kernel(lanes, parts, *refs):
    acts, taken, (hidden, dgate, dup, pg, cot) = refs[:parts], refs[parts : 2 * parts], refs[2 * parts :]
    ff, width = hidden.shape[1], pg.shape[1]
    start = 0
    for act, rows in zip(acts, taken):
        at = slice(start, start + act.shape[0])
        start += act.shape[0]
        for j, out in enumerate((hidden, dgate, dup)):
            out[at, :] = act[:, j * lanes : j * lanes + ff]
        pg[at, :] = rows[:, :width]
        cot[at, :] = rows[:, width:]


def grad_kernel(tile, count, *refs):
    lefts, rights, outs, buffers, (sem,) = (refs[i * count : (i + 1) * count] for i in range(5))
    copies = []
    for left, right, out, buffer in zip(lefts, rights, outs, buffers):
        for start in range(0, left.shape[1], tile):
            at = slice(start, min(start + tile, left.shape[1]))
            buffer[at, :] = lax.dot_general(
                left[:, at], right[...], (((0,), (0,)), ((), ())), preferred_element_type=f32
            )
            copy = pltpu.make_async_copy(buffer.at[at, :], out.at[at, :], sem.at[len(copies)])
            copy.start()
            copies.append(copy)
    for copy in copies:
        copy.wait()


def last_kernel(want, picked, taken, mixed, cot, router, gain, *refs):
    *blocks, updated_ref, grad_ref = refs
    _, width = cot.shape
    sums = blocks[0][...].astype(f32)
    for block in blocks[1:]:
        sums = sums + block[...].astype(f32)
    scalars = sums[:, 2 * width :]
    kind = lax.broadcasted_iota(jnp.int32, scalars.shape, 1) % (2 * PARTS)
    dlogit = jnp.sum(jnp.where(kind < PARTS, scalars, 0.0), axis=1, keepdims=True)
    inner = jnp.sum(jnp.where(kind < PARTS, 0.0, scalars), axis=1, keepdims=True)
    new_rows = (picked[...] + sums[:, :width]).astype(bf16)
    drows = (
        taken[: picked.shape[0], width:].astype(f32)
        + sums[:, width : 2 * width] * gain[...].astype(f32)
        - picked[...] * inner
        + dlogit * router[...].astype(f32)
    ).astype(bf16)
    updated_ref[...] = (mixed[...].astype(f32) + dot_nn(want[...], new_rows)).astype(bf16)
    grad_ref[...] = (cot[...].astype(f32) + dot_nn(want[...], drows)).astype(bf16)


def fast(states, mix_weights, router, norm_gain, gate_weight, up_weight, down_weight, counts, chosen, cotangent):
    slots = lax.axis_size("dp")
    tensor = lax.axis_size("tensor")
    cap = chosen.shape[1]
    tokens, width = cotangent.shape
    ff = gate_weight.shape[1]
    model_width = width * tensor
    lanes = (ff + 2 * PARTS * tensor + 127) // 128 * 128
    columns = 2 * width + 128
    hbm = pl.BlockSpec(memory_space=pltpu.HBM)
    anywhere = pl.BlockSpec(memory_space=pl.ANY)
    block = sds((cap, columns), bf16)

    def over_dp(x, k):
        return lax.ppermute(x, "dp", [(i, i ^ k) for i in range(slots)])

    def over_tensor(x, k):
        return lax.ppermute(x, "tensor", [(i, i ^ k) for i in range(tensor)])

    def copy_of(x, space=pltpu.VMEM):
        return space(x.shape, x.dtype)

    sem = pltpu.SemaphoreType.DMA((8,))
    picked, load = call(
        functools.partial(pick_kernel, cap),
        (sds((cap, width), f32), block),
        [hbm] * 7,
        [copy_of(x, pltpu.SMEM) for x in (counts, chosen, mix_weights)]
        + [copy_of(x) for x in (states, cotangent, router, norm_gain)]
        + [sem],
        vmem=65_000_000,
    )(counts, chosen, mix_weights, states, cotangent, router, norm_gain)
    blocks = {0: load}
    for step in (4, 2, 1):
        for k in list(blocks):
            blocks[k ^ step] = over_dp(blocks[k], step)
    weight = sds((ff, width), bf16)
    weights = call(
        weights_kernel, (weight,) * 3, [hbm] * 3, [sem], nbytes=13 << 20, vmem=48_000_000,
    )(gate_weight.T, up_weight.T, down_weight)
    mixed, cot_kept, want = call(
        prep_kernel,
        (sds((tokens, width), bf16), sds((tokens, width), bf16), sds((tokens, cap), bf16)),
        [hbm] * 5,
        [copy_of(x, pltpu.SMEM) for x in (counts, chosen, mix_weights)] + [copy_of(states), copy_of(cotangent), sem],
        nbytes=3 << 20,
    )(counts, chosen, mix_weights, states, cotangent)

    def summed(chosen_slots):
        part = len(chosen_slots)
        rows, half = part * cap, part * cap // 2
        own, send, taken = call(
            functools.partial(first_kernel, part, lanes),
            (sds((half, 3 * lanes), f32), sds((half, 3 * lanes), bf16), sds((rows, 2 * width), bf16)),
            [VMEM] * (part + 3),
            [pltpu.VMEM((rows, 3 * lanes), f32)],
        )(*[blocks[k] for k in chosen_slots], *weights)
        send, own = call(
            add_kernel, (sds((half, 3 * lanes), bf16), sds((half, 3 * lanes), f32)), [VMEM] * 2
        )(own, over_tensor(send, 1))
        return own, over_tensor(send, 2), taken

    def acted(part, own, got):
        act = call(
            functools.partial(act_kernel, ff, lanes, model_width), sds(got.shape, bf16), [VMEM] * 2
        )(own, got)
        *some, act = call(
            functools.partial(second_kernel, part, lanes),
            tuple([block] * part + [sds((part * cap, 3 * lanes), bf16)]),
            [VMEM] * 5,
        )(act, over_tensor(act, 1), *weights)
        return some, act

    chunks = {"n": (0, 1, 2, 3), "m": (4, 5), "f": (6, 7)}
    sums = {name: summed(some) for name, some in chunks.items()}
    outs, acts, taken = [], [], []
    for name, some in chunks.items():
        own, got, rows_of = sums[name]
        blocks_of, act = acted(len(some), own, got)
        outs += blocks_of
        acts.append(act)
        taken.append(rows_of)

    def moved(value, step):
        return over_dp(value, step).astype(f32)

    def total_of(k, *more):
        return sum(more, outs[k].astype(f32) + moved(outs[k ^ 1], 1)).astype(bf16)

    sum_4 = total_of(4, moved(total_of(6), 2))
    back = [over_dp(outs[1], 1), over_dp(total_of(2), 2), over_dp(sum_4, 4)]
    hidden, dgate, dup, pg, cot = call(
        functools.partial(join_kernel, lanes, len(chunks)),
        tuple([sds((slots * cap, ff), bf16)] * 3 + [sds((slots * cap, width), bf16)] * 2),
        [VMEM] * (2 * len(chunks)),
    )(*acts, *taken)
    tile = 256

    def grads(lefts, rights):
        out = sds((ff, width), f32)
        count = len(lefts)
        return pl.pallas_call(
            functools.partial(grad_kernel, tile, count),
            out_shape=(out,) * count,
            in_specs=[VMEM] * (2 * count),
            out_specs=(anywhere,) * count,
            scratch_shapes=[pltpu.VMEM(out.shape, f32)] * count
            + [pltpu.SemaphoreType.DMA((count * pl.cdiv(ff, tile),))],
            compiler_params=pltpu.CompilerParams(vmem_limit_bytes=32 << 20),
            cost_estimate=pl.CostEstimate(flops=0, bytes_accessed=count * ff * width * 4, transcendentals=0),
        )(*lefts, *rights)

    (grad_down,) = grads((hidden,), (cot,))
    grad_gate, grad_up = (grad.T for grad in grads((dgate, dup), (pg, pg)))
    updated, grad_input = call(
        last_kernel, (sds((tokens, width), bf16), sds((tokens, width), bf16)), [VMEM] * 11
    )(want, picked, taken[0], mixed, cot_kept, router.reshape(1, width), norm_gain.reshape(1, width), outs[0], *back)
    return updated, grad_input, grad_gate, grad_up, grad_down


def general(
    states,
    mix_weights,
    router,
    norm_gain,
    gate_weight,
    up_weight,
    down_weight,
    counts,
    chosen,
    cotangent,
):
    width_here = cotangent.shape[1]
    my_rank = lax.axis_index("dp")
    model_width = width_here * lax.axis_size("tensor")
    mixed = jnp.tensordot(mix_weights, states.astype(jnp.float32), axes=1)
    flat_counts = counts.reshape(-1)
    my_count = flat_counts[my_rank]
    positions = chosen[0]
    capacity = positions.shape[0]
    slot_ids = jnp.arange(capacity, dtype=jnp.int32)
    is_valid = slot_ids < my_count
    valid = is_valid.astype(jnp.float32)[:, None]
    picked = mixed[positions]
    router_float = router.astype(jnp.float32)
    gain_float = norm_gain.astype(jnp.float32)
    logit_part = jnp.sum(picked * router_float, axis=1)
    square_part = jnp.sum(picked * picked, axis=1)
    logits, squares = lax.psum((logit_part, square_part), "tensor")
    gating = jax.nn.sigmoid(logits)
    inverse = lax.rsqrt(squares / model_width + epsilon)
    normed = (picked * inverse[:, None] * gain_float * valid).astype(jnp.bfloat16)
    gathered = lax.all_gather(normed, "dp", axis=0, tiled=True)
    gate_part = jnp.dot(gathered, gate_weight, preferred_element_type=jnp.float32)
    up_part = jnp.dot(gathered, up_weight, preferred_element_type=jnp.float32)
    gate_pre, up_pre = lax.psum((gate_part, up_part), "tensor")
    hidden = (jax.nn.silu(gate_pre) * up_pre).astype(jnp.bfloat16)
    update_work = lax.psum_scatter(
        jnp.dot(hidden, down_weight, preferred_element_type=jnp.float32),
        "dp",
        scatter_dimension=0,
        tiled=True,
    ).astype(jnp.bfloat16)
    update_float = update_work.astype(jnp.float32) * valid
    new_rows = picked + gating[:, None] * update_float
    result = mixed.at[positions].set(new_rows).astype(jnp.bfloat16)
    cot_rows = cotangent[positions].astype(jnp.float32)
    dupdate = (gating[:, None] * cot_rows * valid).astype(jnp.bfloat16)
    dlogit_part = jnp.sum(cot_rows * update_float, axis=1)
    dgathered = lax.all_gather(dupdate, "dp", axis=0, tiled=True)
    dhidden_part = jnp.dot(dgathered, down_weight.T, preferred_element_type=jnp.float32)
    dhidden = lax.psum(dhidden_part, "tensor")
    sigmoid_pre = jax.nn.sigmoid(gate_pre)
    dgate_pre = (dhidden * up_pre * sigmoid_pre * (1.0 + gate_pre * (1.0 - sigmoid_pre))).astype(
        jnp.bfloat16
    )
    dup_pre = (dhidden * gate_pre * sigmoid_pre).astype(jnp.bfloat16)
    grad_down = jnp.dot(hidden.T, dgathered, preferred_element_type=jnp.float32)
    grad_gate = jnp.dot(gathered.T, dgate_pre, preferred_element_type=jnp.float32)
    grad_up = jnp.dot(gathered.T, dup_pre, preferred_element_type=jnp.float32)
    first_term = jnp.dot(dgate_pre, gate_weight.T, preferred_element_type=jnp.float32)
    dnormed_work = lax.psum_scatter(
        first_term + jnp.dot(dup_pre, up_weight.T, preferred_element_type=jnp.float32),
        "dp",
        scatter_dimension=0,
        tiled=True,
    )
    scaled = dnormed_work * gain_float * valid
    inner_part = jnp.sum(scaled * picked, axis=1)
    dlogit_sum, inner_sum = lax.psum((dlogit_part, inner_part), "tensor")
    dlogit = dlogit_sum * gating * (1.0 - gating)
    drows = (
        cot_rows
        + inverse[:, None] * scaled
        - picked * (inverse**3 * inner_sum / model_width)[:, None]
        + valid * dlogit[:, None] * router_float
    )
    grad_input = cotangent.astype(jnp.float32).at[positions].set(drows).astype(jnp.bfloat16)
    return (result, grad_input, grad_gate, grad_up, grad_down)


def solution(mesh):
    small = (mesh.shape["dp"], mesh.shape["tensor"]) == (8, 4)
    return jax.shard_map(
        fast if small else general,
        mesh=mesh,
        in_specs=(
            P(None, "dp", "tensor"),
            P(),
            P("tensor"),
            P("tensor"),
            P("tensor", "dp"),
            P("tensor", "dp"),
            P("dp", "tensor"),
            P(),
            P("dp", None),
            P("dp", "tensor"),
        ),
        out_specs=(
            P("dp", "tensor"),
            P("dp", "tensor"),
            P("tensor", "dp"),
            P("tensor", "dp"),
            P("dp", "tensor"),
        ),
        check_vma=False,
    )
```
